32 devices in a mesh: lon: 8 (over z, core), mem: 4 (over y, x).
Axes of the slice: x: 2, y: 2, z: 4, core: 2. Of those that a mesh axis runs over, the one named last changes fastest.
Arguments:
- members: float32 [32, 4, 192, 256], P('mem', None, 'lon'), may hold values from -6 to 6
- courant_lon: float32 [4, 192, 256], P(None, 'lon'), may hold values from -0.55 to 0.55
- courant_lat: float32 [4, 192, 256], P(None, 'lon'), may hold values from -0.4 to 0.4
- vert_modes: float32 [2, 4], replicated, may hold values from -1 to 1
- horiz_modes: float32 [4, 192, 256], P(None, 'lon'), may hold values from -1 to 1
- obs_index: int32 [16384], P('lon'), may hold values from 0 to 24575
- obs_count: int32 [8], P('lon'), may hold values from 1024 to 2048, as said below
- obs_value: float32 [16384], P('lon'), may hold values from -6 to 6
- obs_var: float32 [16384], P('lon'), may hold values from 2 to 48
Outputs:
- prior_trajectories: float32 [32, 4, 192, 256], P('mem', None, 'lon')
- analysis_mean: float32 [4, 192, 256], P(None, 'lon')
The draws below stay inside these ranges and needn't reach their ends.
Inputs may be any that keep to these rules, and one draw needn't show every extreme that they name: `obs_index`: index of a cell within the band's own block: level, then longitude within the band, then latitude. Each band uses its first obs_count slots; some band uses all 2048.
All inputs are finite; a program needn't handle non-finite values.
Results may differ from the reference program's by a relative error of at most 0.0001.
Values sent between devices are 32-bit elements; how exact they have to be, the bound alone decides.
A program may use at most 128 MiB of HBM per device.

```python
import math
import jax
import jax.numpy as jnp
from jax import lax

LON_DEV = 24
NLAT = 256
L = 4
KV = 2
KH = 4
ADV_STEPS = 2
OBS_DEV = 2048
NLON = 192
BANDS = 8
MEMBERS = 32
NOBS = 16384


def draw_obs_count(key, part):
    key_count, key_full = jax.random.split(key)
    counts = jax.random.randint(key_count, (BANDS,), OBS_DEV // 2, OBS_DEV + 1)
    full_band = jax.random.randint(key_full, (), 0, BANDS)
    return jnp.where(jnp.arange(BANDS) == full_band, OBS_DEV, counts).astype(jnp.int32)


def draw_obs_var(key, part):
    band_pos = (jnp.arange(NOBS) // OBS_DEV).astype(jnp.float32)
    rise_factor = 1.0 + 2.0 * band_pos / max(BANDS - 1, 1)
    spread = jnp.exp(jax.random.uniform(key, (NOBS,), jnp.float32, math.log(2.0), math.log(16.0)))
    return (rise_factor * spread).astype(jnp.float32)


def set_ends(values, rng, least, largest):
    place = [jax.random.randint(jax.random.fold_in(rng, axis), (), 0, length) for axis, length in enumerate(values.shape)]
    main_axis = values.shape.index(max(values.shape))
    next_to = place[:main_axis] + [(place[main_axis] + 1) % values.shape[main_axis]] + place[main_axis + 1:]
    return values.at[tuple(place)].set(least).at[tuple(next_to)].set(largest)


def block_scale(own_key, dims, pieces, low, high):
    def one(position, shards_of):
        draws = jax.random.uniform(jax.random.fold_in(jax.random.fold_in(own_key, 6), position), (shards_of,), jnp.float32, low / len(pieces), high / len(pieces))
        return jnp.repeat(jnp.exp(draws), dims[position] // shards_of).reshape((-1,) + (1,) * (len(dims) - position - 1))

    level = one(*pieces[0])
    for cut in pieces[1:]:
        level = level * one(*cut)
    return level


def normal_values(stream_key, extent, width, bound, pieces=(), kind=jnp.bfloat16):
    values = jax.random.normal(stream_key, extent, jnp.float32) * width
    if len(pieces) > 0:
        values = block_scale(stream_key, extent, pieces, -0.22, 0.18) * values
    return jnp.clip(values, min=-bound, max=bound).astype(kind)


def setup_inputs(seed: int = 0) -> dict:
    arg_keys = jax.random.split(jax.random.key(seed), 10)
    return {
        "members": normal_values(arg_keys[0], (MEMBERS, L, NLON, NLAT), 1.0, 6.0, ((0, 4), (2, 8)), jnp.float32),
        "courant_lon": jnp.clip(jax.random.uniform(arg_keys[1], (L, NLON, NLAT), jnp.float32, -0.55, 0.55) * block_scale(arg_keys[1], (L, NLON, NLAT), ((1, 8),), -0.4, 0.0), -0.55, 0.55),
        "courant_lat": jnp.clip(jax.random.uniform(arg_keys[2], (L, NLON, NLAT), jnp.float32, -0.4, 0.4) * block_scale(arg_keys[2], (L, NLON, NLAT), ((1, 8),), -0.4, 0.0), -0.4, 0.4),
        "vert_modes": jnp.clip(jax.random.uniform(arg_keys[3], (KV, L), jnp.float32, -1.0, 1.0), -1.0, 1.0),
        "horiz_modes": jnp.clip(jax.random.uniform(arg_keys[4], (KH, NLON, NLAT), jnp.float32, -1.0, 1.0) * block_scale(arg_keys[4], (KH, NLON, NLAT), ((1, 8),), -0.4, 0.0), -1.0, 1.0),
        "obs_index": set_ends(jax.random.randint(arg_keys[5], (NOBS,), 0, L * LON_DEV * NLAT), jax.random.fold_in(arg_keys[5], 1), 0, (L * LON_DEV * NLAT) - 1).astype(jnp.int32),
        "obs_count": draw_obs_count(jax.random.fold_in(arg_keys[9], 71), 0),
        "obs_value": normal_values(arg_keys[7], (NOBS,), 1.0, 6.0, ((0, 8),), jnp.float32),
        "obs_var": draw_obs_var(jax.random.fold_in(arg_keys[9], 71), 0),
    }


def update(centre, western, eastern, flow_lon, flow_lat):
    zero_col = jnp.zeros_like(centre[..., :1])
    south_boundary = jnp.concatenate([zero_col, centre[..., :-1]], axis=-1)
    northern = jnp.concatenate([centre[..., 1:], zero_col], axis=-1)
    result = centre - jnp.maximum(flow_lon, 0.0) * (centre - western)
    result = result - jnp.minimum(flow_lon, 0.0) * (eastern - centre)
    result = result - jnp.maximum(flow_lat, 0.0) * (centre - south_boundary)
    result = result - jnp.minimum(flow_lat, 0.0) * (northern - centre)
    return result

def reference(members, courant_lon, courant_lat, vert_modes, horiz_modes, obs_index, obs_count, obs_value, obs_var):
    prognostic_vector = members
    for section in range(ADV_STEPS):
        prognostic_vector = update(prognostic_vector, jnp.roll(prognostic_vector, 1, axis=2), jnp.roll(prognostic_vector, -1, axis=2), courant_lon, courant_lat)
    prior_trajectories = prognostic_vector
    sample_tally_overall = members.shape[0]
    lat_rows = members.shape[3]
    sample_centroid = jnp.sum(prior_trajectories, axis=0) / sample_tally_overall
    sample_departure = prior_trajectories - sample_centroid[None]
    norm_scale = (sample_tally_overall - 1) ** (-0.5)
    obs_slots = obs_index.shape[0]
    slot_idx = jnp.arange(obs_slots, dtype=jnp.int32)
    band_idx = slot_idx // OBS_DEV
    band_cells = LON_DEV * lat_rows
    level_idx = obs_index // band_cells
    within = obs_index % band_cells
    lon_global = band_idx * LON_DEV + within // lat_rows
    lat_idx = within % lat_rows
    anomaly_obs = sample_departure[:, level_idx, lon_global, lat_idx]
    mean_obs = sample_centroid[level_idx, lon_global, lat_idx]
    vert_obs = vert_modes[:, level_idx]
    horiz_obs = horiz_modes[:, lon_global, lat_idx]
    modes_obs = (vert_obs[:, None, :] * horiz_obs[None, :, :]).reshape(KV * KH, obs_slots)
    live_mask = (slot_idx % OBS_DEV < obs_count[band_idx]).astype(jnp.float32)
    obs_perts = anomaly_obs[:, None, :] * modes_obs[None, :, :] * (live_mask * norm_scale)[None, None, :]
    obs_perts = obs_perts.reshape(sample_tally_overall * KV * KH, obs_slots)
    inv_var = live_mask / obs_var
    innovation = obs_value - mean_obs
    gram_matrix = jnp.dot(obs_perts * inv_var[None, :], obs_perts.T, precision=lax.Precision.HIGHEST)
    right_side = jnp.dot(obs_perts, inv_var * innovation, precision=lax.Precision.HIGHEST)
    system = jnp.eye(gram_matrix.shape[0], dtype=jnp.float32) + gram_matrix
    factor = jnp.linalg.cholesky(system)
    weights = jax.scipy.linalg.cho_solve((factor, True), right_side)
    w_mat = weights.reshape(sample_tally_overall, KV * KH)
    mode_coef = jnp.einsum('mk,mlij->klij', w_mat, sample_departure, precision=lax.Precision.HIGHEST)
    mode_coef = mode_coef.reshape(KV, KH, mode_coef.shape[1], mode_coef.shape[2], mode_coef.shape[3])
    posterior_adjustment = jnp.einsum('al,bij,ablij->lij', vert_modes, horiz_modes, mode_coef, precision=lax.Precision.HIGHEST) * norm_scale
    return (prior_trajectories, sample_centroid + posterior_adjustment)
```

```python
import functools

import jax
import jax.numpy as jnp
from jax import lax
from jax.experimental import pallas as pl
from jax.experimental.pallas import tpu as pltpu
from jax.sharding import PartitionSpec as P

KV = 2
KH = 4
ADV_STEPS = 2
MODES = KV * KH
MESH = pl.DeviceIdType.MESH
VMEM_LIMIT = 56 * 1024 * 1024
HIGHEST = lax.Precision.HIGHEST


def vmem():
    return pl.BlockSpec(memory_space=pltpu.VMEM)


def smem():
    return pl.BlockSpec(memory_space=pltpu.SMEM)


def greet(peers):
    barrier = pltpu.get_barrier_semaphore()
    for peer in peers:
        pl.semaphore_signal(barrier, inc=1, device_id=peer, device_id_type=MESH)
    pl.semaphore_wait(barrier, len(peers))


def axis_peers(axis, count):
    me = lax.axis_index(axis)
    return [{axis: lax.rem(me + d, count)} for d in range(1, count)]


def send(src, dst, send_sem, recv_sem, peer):
    copy = pltpu.make_async_remote_copy(
        src_ref=src, dst_ref=dst, send_sem=send_sem, recv_sem=recv_sem,
        device_id=peer, device_id_type=MESH,
    )
    copy.start()
    return copy


def advect_kernel(
    n_lon, n_mem, mem_dev,
    members, cx, cy, horiz, level, within,
    prior, mean, obs_prior, obs_horiz,
    edge_out, edge_in, ext, cx_ext, cy_ext, partial, cols, table, picked, gathered,
    edge_send, edge_recv, mean_send, mean_recv, obs_send, obs_recv,
):
    layers = cx.shape[0]
    stack, width, lats = members.shape
    rows = 40
    halves = lats // 128
    me = lax.axis_index("lon")
    me_mem = lax.axis_index("mem")
    left = {"lon": lax.rem(me + n_lon - 1, n_lon)}
    right = {"lon": lax.rem(me + 1, n_lon)}
    others = axis_peers("mem", n_mem)

    for side, (first, second, rim) in enumerate(((0, 1, 0), (width - 2, width - 1, width - 1))):
        edge_out[side, 0:stack, :] = members[:, first, :]
        edge_out[side, stack : 2 * stack, :] = members[:, second, :]
        edge_out[side, 2 * stack : 2 * stack + layers, :] = cx[:, rim, :]
        edge_out[side, 2 * stack + layers : 2 * stack + 2 * layers, :] = cy[:, rim, :]
    greet([left, right] + others)
    to_left = send(edge_out.at[0], edge_in.at[1], edge_send.at[0], edge_recv.at[1], left)
    to_right = send(edge_out.at[1], edge_in.at[0], edge_send.at[1], edge_recv.at[0], right)

    ext[:, 4 : 4 + width, :] = members[...]
    cx_ext[:, 4 : 4 + width, :] = cx[...]
    cy_ext[:, 4 : 4 + width, :] = cy[...]
    for b in range(2 * KH):
        for h in range(halves):
            cols[h, pl.ds(stack + b, width, stride=rows), :] = horiz[
                b % KH, :, h * 128 : (h + 1) * 128
            ]
    to_left.wait_recv()
    to_right.wait_recv()
    high = 4 + width
    ext[:, 2, :] = edge_in[0, 0:stack, :]
    ext[:, 3, :] = edge_in[0, stack : 2 * stack, :]
    ext[:, high, :] = edge_in[1, 0:stack, :]
    ext[:, high + 1, :] = edge_in[1, stack : 2 * stack, :]
    for side, row in ((0, 3), (1, high)):
        cx_ext[:, row, :] = edge_in[side, 2 * stack : 2 * stack + layers, :]
        cy_ext[:, row, :] = edge_in[side, 2 * stack + layers : 2 * stack + 2 * layers, :]

    ext_rows = width + 8
    lane = lax.broadcasted_iota(jnp.int32, (ext_rows, lats), 1)
    for l in range(layers):
        cx_l = cx_ext[l]
        cy_l = cy_ext[l]
        east_flow = jnp.maximum(cx_l, 0.0)
        west_flow = jnp.minimum(cx_l, 0.0)
        north_flow = jnp.maximum(cy_l, 0.0)
        south_flow = jnp.minimum(cy_l, 0.0)

        def step(m, total, l=l, flows=(east_flow, west_flow, north_flow, south_flow)):
            q = ext[m * layers + l]
            for _ in range(ADV_STEPS):
                qw = pltpu.roll(q, 1, 0)
                qe = pltpu.roll(q, ext_rows - 1, 0)
                qs = jnp.where(lane == 0, 0.0, pltpu.roll(q, 1, 1))
                qn = jnp.where(lane == lats - 1, 0.0, pltpu.roll(q, lats - 1, 1))
                r = q - flows[0] * (q - qw)
                r = r - flows[1] * (qe - q)
                r = r - flows[2] * (q - qs)
                q = r - flows[3] * (qn - q)
            inner = q[4 : 4 + width, :]
            prior[m * layers + l] = inner
            for h in range(halves):
                cols[h, pl.ds(l * mem_dev + m, width, stride=rows), :] = inner[
                    :, h * 128 : (h + 1) * 128
                ]
            return total + inner

        total = lax.fori_loop(0, mem_dev, step, jnp.zeros((width, lats), jnp.float32))
        partial[me_mem, l] = total

    mean_copies = [
        send(partial.at[me_mem], partial.at[me_mem], mean_send.at[d], mean_recv.at[d], peer)
        for d, peer in enumerate(others)
    ]

    def turn(i, carry):
        for h in range(halves):
            block = cols[h, pl.ds(pl.multiple_of(i * rows, 8), rows), :]
            start = pl.multiple_of(i * lats + h * 128, 128)
            table[pl.ds(start, 128), 0:rows] = block.T
        return carry

    lax.fori_loop(0, width, turn, 0)

    slots = within.shape[0]
    unroll = 16

    def fetch(g, carry):
        for u in range(unroll):
            o = g * unroll + u
            picked[pl.ds(o, 1), :] = table[pl.ds(within[o], 1), :]
        return carry

    lax.fori_loop(0, slots // unroll, fetch, 0)

    def sort_out(c, carry):
        start = pl.multiple_of(c * 128, 128)
        block = picked[pl.ds(start, 128), :].T
        lev = level[:, pl.ds(start, 128)]
        value = block[0:mem_dev]
        for l in range(1, layers):
            value = jnp.where(lev == l, block[l * mem_dev : (l + 1) * mem_dev], value)
        gathered[me_mem, :, pl.ds(start, 128)] = value
        obs_horiz[:, pl.ds(start, 128)] = block[stack : stack + 8]
        return carry

    lax.fori_loop(0, slots // 128, sort_out, 0)
    obs_copies = [
        send(gathered.at[me_mem], gathered.at[me_mem], obs_send.at[d], obs_recv.at[d], peer)
        for d, peer in enumerate(others)
    ]
    for copy in mean_copies:
        copy.wait_recv()
    field = partial[0]
    for g in range(1, n_mem):
        field = field + partial[g]
    mean[...] = field / (n_mem * mem_dev)
    for copy in obs_copies:
        copy.wait_recv()
    obs_prior[...] = gathered[...]
    to_left.wait_send()
    to_right.wait_send()
    for copy in mean_copies + obs_copies:
        copy.wait_send()


def gram_kernel(
    n_lon, n_mem, mem_dev, norm,
    obs_prior, obs_horiz, level, vert, count, value, var,
    system,
    perts, weighted, staged, heard, whole,
    part_send, part_recv, lon_send, lon_recv, mem_send, mem_recv,
):
    slots = level.shape[1]
    layers = vert.shape[1]
    total = n_mem * mem_dev
    local = mem_dev * MODES
    size = total * MODES
    me = lax.axis_index("lon")
    me_mem = lax.axis_index("mem")
    lon_peers = axis_peers("lon", n_lon)
    mem_peers = axis_peers("mem", n_mem)

    lev = level[...]
    states = obs_prior[...].reshape(total, slots)
    centre = jnp.sum(states, axis=0, keepdims=True) / total
    slot = lax.broadcasted_iota(jnp.int32, (1, slots), 1)
    live = jnp.where(slot < count[0], 1.0, 0.0)
    inv_var = live / var[...]
    drive = inv_var * (value[...] - centre)
    scale = live * norm
    vert_obs = []
    for a in range(KV):
        v = jnp.full((1, slots), vert[a, 0])
        for l in range(1, layers):
            v = jnp.where(lev == l, vert[a, l], v)
        vert_obs.append(jnp.broadcast_to(v, (KH, slots)))
    modes = jnp.concatenate(vert_obs, axis=0) * obs_horiz[...]
    for g in range(n_mem):
        for m in range(mem_dev):
            row = (g * mem_dev + m) * MODES
            anomaly = obs_prior[g, m : m + 1, :] - centre
            perts[row : row + MODES, :] = anomaly * modes * scale
    start = pl.multiple_of(me_mem * local, local)
    mine = perts[pl.ds(start, local), :]
    weighted[...] = mine * inv_var
    gram = lax.dot_general(
        weighted[...], perts[...], (((1,), (1,)), ((), ())),
        precision=HIGHEST, preferred_element_type=jnp.float32,
    )
    side = jnp.sum(mine * drive, axis=1, keepdims=True)
    for d in range(n_lon):
        staged[d, :, 0:size] = gram[d * 8 : (d + 1) * 8]
        staged[d, :, size : size + 128] = jnp.broadcast_to(side[d * 8 : (d + 1) * 8], (8, 128))

    greet(lon_peers + mem_peers)
    parts = []
    for d, peer in enumerate(lon_peers):
        parts.append(
            send(staged.at[peer["lon"]], heard.at[me], part_send.at[d], part_recv.at[d], peer)
        )
    heard[me] = staged[me]
    for copy in parts:
        copy.wait_recv()
    block = heard[0]
    for d in range(1, n_lon):
        block = block + heard[d]
    whole[me_mem, me] = block
    spread = [
        send(whole.at[me_mem, me], whole.at[me_mem, me], lon_send.at[d], lon_recv.at[d], peer)
        for d, peer in enumerate(lon_peers)
    ]
    for copy in spread:
        copy.wait_recv()
    across = [
        send(whole.at[me_mem], whole.at[me_mem], mem_send.at[d], mem_recv.at[d], peer)
        for d, peer in enumerate(mem_peers)
    ]
    for copy in across:
        copy.wait_recv()
    system[...] = whole[...].reshape(size, size + 128)
    for copy in parts + spread + across:
        copy.wait_send()


def solve_kernel(system, weights, work, pivot, strip):
    size, columns = system.shape
    row = lax.broadcasted_iota(jnp.int32, (size, columns), 0)
    col = lax.broadcasted_iota(jnp.int32, (size, columns), 1)
    work[...] = system[...] + jnp.where(row == col, 1.0, 0.0)
    for group in range(size // 128):
        low = group * 128
        left = columns - low

        def panel(p, carry, low=low, left=left):
            base = pl.multiple_of(low + p * 8, 8)
            shift = lax.rem(128 - p * 8, 128)
            head = pltpu.roll(work[pl.ds(base, 8), low : low + 128], shift, 1)
            pivot[...] = head
            strip[...] = work[pl.ds(base, 8), :]
            a = [
                [jnp.broadcast_to(pivot[r : r + 1, c : c + 1], (1, 128)) for c in range(8)]
                for r in range(8)
            ]
            rows = [
                [strip[r : r + 1, low + k * 128 : low + (k + 1) * 128] for k in range(left // 128)]
                for r in range(8)
            ]
            for j in range(8):
                inv = 1.0 / a[j][j]
                for c in range(j + 1, 8):
                    a[j][c] = a[j][c] * inv
                rows[j] = [x * inv for x in rows[j]]
                for r in range(8):
                    if r != j:
                        f = a[r][j]
                        for c in range(j + 1, 8):
                            a[r][c] = a[r][c] - f * a[j][c]
                        rows[r] = [x - f * y for x, y in zip(rows[r], rows[j])]
            spread = [[jnp.broadcast_to(x, (8, 128)) for x in rows[r]] for r in range(8)]
            for i in range(size // 8):
                block = [work[i * 8 : i * 8 + 8, low + k * 128 : low + (k + 1) * 128] for k in range(left // 128)]
                lead = pltpu.roll(block[0], shift, 1)
                for j in range(8):
                    f = jnp.broadcast_to(lead[:, j : j + 1], (8, 128))
                    block = [x - f * y for x, y in zip(block, spread[j])]
                for k in range(left // 128):
                    work[i * 8 : i * 8 + 8, low + k * 128 : low + (k + 1) * 128] = block[k]
            for r in range(8):
                for k in range(left // 128):
                    strip[r : r + 1, low + k * 128 : low + (k + 1) * 128] = rows[r][k]
            work[pl.ds(base, 8), low:columns] = strip[:, low:columns]
            return carry

        lax.fori_loop(0, 16, panel, 0)
    weights[...] = work[:, size : size + 128]


def analysis_kernel(
    n_mem, mem_dev, norm,
    weights, prior, mean, horiz, vert,
    analysis,
    partial, part_send, part_recv,
):
    layers = vert.shape[1]
    lats = mean.shape[2]
    me_mem = lax.axis_index("mem")
    peers = axis_peers("mem", n_mem)
    for l in range(layers):
        centre = mean[l]
        total = jnp.zeros_like(centre)
        for m in range(mem_dev):
            start = pl.multiple_of((me_mem * mem_dev + m) * MODES, 8)
            w = weights[pl.ds(start, MODES), :]
            mixed = vert[0, l] * w[0:KH] + vert[1, l] * w[KH : 2 * KH]
            mixed = jnp.concatenate([mixed] * (lats // 128), axis=1)
            coef = mixed[0:1] * horiz[0]
            for b in range(1, KH):
                coef = coef + mixed[b : b + 1] * horiz[b]
            total = total + coef * (prior[m * layers + l] - centre)
        partial[me_mem, l] = total
    greet(peers)
    copies = [
        send(partial.at[me_mem], partial.at[me_mem], part_send.at[d], part_recv.at[d], peer)
        for d, peer in enumerate(peers)
    ]
    for copy in copies:
        copy.wait_recv()
    field = partial[0]
    for g in range(1, n_mem):
        field = field + partial[g]
    analysis[...] = mean[...] + field * norm
    for copy in copies:
        copy.wait_send()


def params(collective=None):
    if collective is None:
        return pltpu.CompilerParams(vmem_limit_bytes=VMEM_LIMIT)
    return pltpu.CompilerParams(
        vmem_limit_bytes=VMEM_LIMIT, collective_id=collective, has_side_effects=True
    )


def fast_device(
    members, courant_lon, courant_lat, vert_modes, horiz_modes,
    obs_index, obs_count, obs_value, obs_var,
):
    f32 = jnp.float32
    mem_dev, layers, width, lats = members.shape
    n_lon = lax.axis_size("lon")
    n_mem = lax.axis_size("mem")
    total = mem_dev * n_mem
    size = total * MODES
    norm = (total - 1) ** (-0.5)
    slots = obs_index.shape[0]
    stack = mem_dev * layers
    cells = width * lats
    level = (obs_index // cells).reshape(1, slots)
    within = obs_index % cells
    dma = pltpu.SemaphoreType.DMA
    halves = lats // 128
    edge_rows = 2 * stack + 2 * layers
    prior, mean, obs_prior, obs_horiz = pl.pallas_call(
        functools.partial(advect_kernel, n_lon, n_mem, mem_dev),
        out_shape=(
            jax.ShapeDtypeStruct((stack, width, lats), f32),
            jax.ShapeDtypeStruct((layers, width, lats), f32),
            jax.ShapeDtypeStruct((n_mem, mem_dev, slots), f32),
            jax.ShapeDtypeStruct((8, slots), f32),
        ),
        in_specs=[vmem()] * 5 + [smem()],
        out_specs=(vmem(),) * 4,
        scratch_shapes=[
            pltpu.VMEM((2, edge_rows, lats), f32),
            pltpu.VMEM((2, edge_rows, lats), f32),
            pltpu.VMEM((stack, width + 8, lats), f32),
            pltpu.VMEM((layers, width + 8, lats), f32),
            pltpu.VMEM((layers, width + 8, lats), f32),
            pltpu.VMEM((n_mem, layers, width, lats), f32),
            pltpu.VMEM((halves, width * 40, 128), f32),
            pltpu.VMEM((cells, 128), f32),
            pltpu.VMEM((slots, 128), f32),
            pltpu.VMEM((n_mem, mem_dev, slots), f32),
            dma((2,)), dma((2,)),
            dma((n_mem - 1,)), dma((n_mem - 1,)),
            dma((n_mem - 1,)), dma((n_mem - 1,)),
        ],
        compiler_params=params(1),
        name="advect",
    )(members.reshape(stack, width, lats), courant_lon, courant_lat, horiz_modes, level, within)
    system = pl.pallas_call(
        functools.partial(gram_kernel, n_lon, n_mem, mem_dev, norm),
        out_shape=jax.ShapeDtypeStruct((size, size + 128), f32),
        in_specs=[vmem()] * 3 + [smem()] * 2 + [vmem()] * 2,
        out_specs=vmem(),
        scratch_shapes=[
            pltpu.VMEM((size, slots), f32),
            pltpu.VMEM((mem_dev * MODES, slots), f32),
            pltpu.VMEM((n_lon, 8, size + 128), f32),
            pltpu.VMEM((n_lon, 8, size + 128), f32),
            pltpu.VMEM((n_mem, n_lon, 8, size + 128), f32),
            dma((n_lon - 1,)), dma((n_lon - 1,)),
            dma((n_lon - 1,)), dma((n_lon - 1,)),
            dma((n_mem - 1,)), dma((n_mem - 1,)),
        ],
        compiler_params=params(2),
        name="gram",
    )(
        obs_prior, obs_horiz, level, vert_modes, obs_count,
        obs_value.reshape(1, slots), obs_var.reshape(1, slots),
    )
    weights = pl.pallas_call(
        solve_kernel,
        out_shape=jax.ShapeDtypeStruct((size, 128), f32),
        in_specs=[vmem()],
        out_specs=vmem(),
        scratch_shapes=[pltpu.VMEM((size, size + 128), f32),
            pltpu.VMEM((8, 128), f32),
            pltpu.VMEM((8, size + 128), f32),
        ],
        compiler_params=params(),
        name="solve",
    )(system)
    analysis = pl.pallas_call(
        functools.partial(analysis_kernel, n_mem, mem_dev, norm),
        out_shape=jax.ShapeDtypeStruct((layers, width, lats), f32),
        in_specs=[vmem()] * 4 + [smem()],
        out_specs=vmem(),
        scratch_shapes=[
            pltpu.VMEM((n_mem, layers, width, lats), f32),
            dma((n_mem - 1,)), dma((n_mem - 1,)),
        ],
        compiler_params=params(3),
        name="analysis",
    )(weights, prior, mean, horiz_modes, vert_modes)
    return prior.reshape(members.shape), analysis


def padded(block, sides, width):
    for axis, dim in sides:
        count = lax.axis_size(axis)
        forward = [(i, i + 1) for i in range(count - 1)]
        forward.append((count - 1, 0))
        backward = [(target, source) for source, target in forward]
        low = lax.ppermute(
            lax.slice_in_dim(block, block.shape[dim] - width, None, axis=dim), axis, forward
        )
        high = lax.ppermute(lax.slice_in_dim(block, 0, width, axis=dim), axis, backward)
        block = jnp.concatenate([low, block, high], axis=dim)
    return block


def update(centre, western, eastern, flow_lon, flow_lat):
    zero_col = jnp.zeros_like(centre[..., :1])
    south_boundary = jnp.concatenate([zero_col, centre[..., :-1]], axis=-1)
    northern = jnp.concatenate([centre[..., 1:], zero_col], axis=-1)
    result = centre - jnp.maximum(flow_lon, 0.0) * (centre - western)
    result = result - jnp.minimum(flow_lon, 0.0) * (eastern - centre)
    result = result - jnp.maximum(flow_lat, 0.0) * (centre - south_boundary)
    result = result - jnp.minimum(flow_lat, 0.0) * (northern - centre)
    return result


def per_device(
    members,
    courant_lon,
    courant_lat,
    vert_modes,
    horiz_modes,
    obs_index,
    obs_count,
    obs_value,
    obs_var,
):
    mem_dev, layer_tally, band_width, lat_rows = members.shape
    sample_tally_overall = mem_dev * lax.axis_size("mem")
    rim_depth = ADV_STEPS
    stacked = jnp.concatenate(
        [members.reshape(mem_dev * layer_tally, band_width, lat_rows), courant_lon, courant_lat],
        axis=0,
    )
    extended = padded(stacked, (("lon", 1),), rim_depth)
    split_at = mem_dev * layer_tally
    prognostic_vector = extended[:split_at].reshape(
        mem_dev, layer_tally, band_width + 2 * rim_depth, lat_rows
    )
    flow_lon_ext = extended[split_at : split_at + layer_tally]
    meridional_wind_padded = extended[split_at + layer_tally :]
    for section in range(rim_depth):
        out_cols = band_width + 2 * (rim_depth - 1 - section)
        first_col = section + 1
        prognostic_vector = update(
            prognostic_vector[:, :, 1 : out_cols + 1],
            prognostic_vector[:, :, 0:out_cols],
            prognostic_vector[:, :, 2 : out_cols + 2],
            flow_lon_ext[:, first_col : first_col + out_cols],
            meridional_wind_padded[:, first_col : first_col + out_cols],
        )
    sample_centroid = lax.psum(jnp.sum(prognostic_vector, axis=0), "mem") / sample_tally_overall
    sample_departure = prognostic_vector - sample_centroid[None]
    norm_scale = (sample_tally_overall - 1) ** (-0.5)
    obs_slots = obs_index.shape[0]
    band_cells = band_width * lat_rows
    level_idx = obs_index // band_cells
    within = obs_index % band_cells
    anomaly_obs = jnp.take(sample_departure.reshape(mem_dev, -1), obs_index, axis=1)
    mean_obs = jnp.take(sample_centroid.reshape(-1), obs_index)
    vert_obs = jnp.take(vert_modes, level_idx, axis=1)
    horiz_obs = jnp.take(horiz_modes.reshape(KH, -1), within, axis=1)
    modes_obs = (vert_obs[:, None, :] * horiz_obs[None, :, :]).reshape(KV * KH, obs_slots)
    live_mask = (jnp.arange(obs_slots, dtype=jnp.int32) < obs_count[0]).astype(jnp.float32)
    obs_perts = (
        anomaly_obs[:, None, :] * modes_obs[None, :, :] * (live_mask * norm_scale)[None, None, :]
    )
    obs_perts = obs_perts.reshape(mem_dev * KV * KH, obs_slots)
    inv_var = live_mask / obs_var
    innovation = obs_value - mean_obs
    all_perts = lax.all_gather(obs_perts, "mem", axis=0, tiled=True)
    gram_part = jnp.dot(all_perts * inv_var[None, :], all_perts.T, precision=lax.Precision.HIGHEST)
    side_part = jnp.dot(all_perts, inv_var * innovation, precision=lax.Precision.HIGHEST)
    gram_matrix, right_side = lax.psum((gram_part, side_part), "lon")
    system = jnp.eye(gram_matrix.shape[0], dtype=jnp.float32) + gram_matrix
    factor = jnp.linalg.cholesky(system)
    weights = jax.scipy.linalg.cho_solve((factor, True), right_side)
    w_mat = weights.reshape(sample_tally_overall, KV * KH)
    w_local = lax.dynamic_slice_in_dim(w_mat, lax.axis_index("mem") * mem_dev, mem_dev, 0)
    mode_coef = jnp.einsum(
        "mk,mlij->klij", w_local, sample_departure, precision=lax.Precision.HIGHEST
    )
    mode_coef = mode_coef.reshape(KV, KH, layer_tally, band_width, lat_rows)
    inc_part = (
        jnp.einsum(
            "al,bij,ablij->lij", vert_modes, horiz_modes, mode_coef, precision=lax.Precision.HIGHEST
        )
        * norm_scale
    )
    posterior_adjustment = lax.psum(inc_part, "mem")
    return (prognostic_vector, sample_centroid + posterior_adjustment)


def choose(*args):
    mem_dev, layers, width, lats = args[0].shape
    n_lon = lax.axis_size("lon")
    fits = (
        mem_dev == 8
        and layers == 4
        and width % 8 == 0
        and lats % 128 == 0
        and args[5].shape[0] % 128 == 0
        and n_lon > 2
        and mem_dev * MODES == 8 * n_lon
        and (mem_dev * lax.axis_size("mem") * MODES) % 128 == 0
    )
    return fast_device(*args) if fits else per_device(*args)


def solution(mesh):
    placed = (
        P("mem", None, "lon", None),
        P(None, "lon", None),
        P(None, "lon", None),
        P(),
        P(None, "lon", None),
        P("lon"),
        P("lon"),
        P("lon"),
        P("lon"),
    )
    return jax.shard_map(
        choose,
        mesh=mesh,
        in_specs=placed,
        out_specs=(P("mem", None, "lon", None), P(None, "lon", None)),
        check_vma=False,
    )
```

```python
import functools

import jax
import jax.numpy as jnp
from jax import lax
from jax.experimental import pallas as pl
from jax.experimental.pallas import tpu as pltpu
from jax.sharding import PartitionSpec as P

KV = 2
KH = 4
ADV_STEPS = 2
MODES = KV * KH
MESH = pl.DeviceIdType.MESH
VMEM_LIMIT = 56 * 1024 * 1024
HIGHEST = lax.Precision.HIGHEST


def vmem():
    return pl.BlockSpec(memory_space=pltpu.VMEM)


def smem():
    return pl.BlockSpec(memory_space=pltpu.SMEM)


def greet(peers):
    barrier = pltpu.get_barrier_semaphore()
    for peer in peers:
        pl.semaphore_signal(barrier, inc=1, device_id=peer, device_id_type=MESH)
    pl.semaphore_wait(barrier, len(peers))


def axis_peers(axis, count):
    me = lax.axis_index(axis)
    return [{axis: lax.rem(me + d, count)} for d in range(1, count)]


def send(src, dst, send_sem, recv_sem, peer):
    copy = pltpu.make_async_remote_copy(
        src_ref=src, dst_ref=dst, send_sem=send_sem, recv_sem=recv_sem,
        device_id=peer, device_id_type=MESH,
    )
    copy.start()
    return copy


def advect_kernel(
    n_lon, n_mem, mem_dev,
    members, cx, cy, horiz, level, within,
    prior, mean, obs_prior, obs_horiz,
    edge_out, edge_in, ext, cx_ext, cy_ext, partial, cols, table, picked, gathered,
    edge_send, edge_recv, mean_send, mean_recv, obs_send, obs_recv,
):
    layers = cx.shape[0]
    stack, width, lats = members.shape
    rows = 40
    halves = lats // 128
    me = lax.axis_index("lon")
    me_mem = lax.axis_index("mem")
    left = {"lon": lax.rem(me + n_lon - 1, n_lon)}
    right = {"lon": lax.rem(me + 1, n_lon)}
    others = axis_peers("mem", n_mem)

    for side, (first, second, rim) in enumerate(((0, 1, 0), (width - 2, width - 1, width - 1))):
        edge_out[side, 0:stack, :] = members[:, first, :]
        edge_out[side, stack : 2 * stack, :] = members[:, second, :]
        edge_out[side, 2 * stack : 2 * stack + layers, :] = cx[:, rim, :]
        edge_out[side, 2 * stack + layers : 2 * stack + 2 * layers, :] = cy[:, rim, :]
    greet([left, right] + others)
    to_left = send(edge_out.at[0], edge_in.at[1], edge_send.at[0], edge_recv.at[1], left)
    to_right = send(edge_out.at[1], edge_in.at[0], edge_send.at[1], edge_recv.at[0], right)

    ext[:, 4 : 4 + width, :] = members[...]
    cx_ext[:, 4 : 4 + width, :] = cx[...]
    cy_ext[:, 4 : 4 + width, :] = cy[...]
    for b in range(2 * KH):
        for h in range(halves):
            cols[h, pl.ds(stack + b, width, stride=rows), :] = horiz[
                b % KH, :, h * 128 : (h + 1) * 128
            ]
    to_left.wait_recv()
    to_right.wait_recv()
    high = 4 + width
    ext[:, 2, :] = edge_in[0, 0:stack, :]
    ext[:, 3, :] = edge_in[0, stack : 2 * stack, :]
    ext[:, high, :] = edge_in[1, 0:stack, :]
    ext[:, high + 1, :] = edge_in[1, stack : 2 * stack, :]
    for side, row in ((0, 3), (1, high)):
        cx_ext[:, row, :] = edge_in[side, 2 * stack : 2 * stack + layers, :]
        cy_ext[:, row, :] = edge_in[side, 2 * stack + layers : 2 * stack + 2 * layers, :]

    ext_rows = width + 8
    lane = lax.broadcasted_iota(jnp.int32, (ext_rows, lats), 1)
    for l in range(layers):
        cx_l = cx_ext[l]
        cy_l = cy_ext[l]
        east_flow = jnp.maximum(cx_l, 0.0)
        west_flow = jnp.minimum(cx_l, 0.0)
        north_flow = jnp.maximum(cy_l, 0.0)
        south_flow = jnp.minimum(cy_l, 0.0)

        def step(m, total, l=l, flows=(east_flow, west_flow, north_flow, south_flow)):
            q = ext[m * layers + l]
            for _ in range(ADV_STEPS):
                qw = pltpu.roll(q, 1, 0)
                qe = pltpu.roll(q, ext_rows - 1, 0)
                qs = jnp.where(lane == 0, 0.0, pltpu.roll(q, 1, 1))
                qn = jnp.where(lane == lats - 1, 0.0, pltpu.roll(q, lats - 1, 1))
                r = q - flows[0] * (q - qw)
                r = r - flows[1] * (qe - q)
                r = r - flows[2] * (q - qs)
                q = r - flows[3] * (qn - q)
            inner = q[4 : 4 + width, :]
            prior[m * layers + l] = inner
            for h in range(halves):
                cols[h, pl.ds(l * mem_dev + m, width, stride=rows), :] = inner[
                    :, h * 128 : (h + 1) * 128
                ]
            return total + inner

        total = lax.fori_loop(0, mem_dev, step, jnp.zeros((width, lats), jnp.float32))
        partial[me_mem, l] = total

    mean_copies = [
        send(partial.at[me_mem], partial.at[me_mem], mean_send.at[d], mean_recv.at[d], peer)
        for d, peer in enumerate(others)
    ]

    def turn(i, carry):
        for h in range(halves):
            block = cols[h, pl.ds(pl.multiple_of(i * rows, 8), rows), :]
            start = pl.multiple_of(i * lats + h * 128, 128)
            table[pl.ds(start, 128), 0:rows] = block.T
        return carry

    lax.fori_loop(0, width, turn, 0)

    slots = within.shape[0]
    unroll = 16

    def fetch(g, carry):
        for u in range(unroll):
            o = g * unroll + u
            picked[pl.ds(o, 1), :] = table[pl.ds(within[o], 1), :]
        return carry

    lax.fori_loop(0, slots // unroll, fetch, 0)

    def sort_out(c, carry):
        start = pl.multiple_of(c * 128, 128)
        block = picked[pl.ds(start, 128), :].T
        lev = level[:, pl.ds(start, 128)]
        value = block[0:mem_dev]
        for l in range(1, layers):
            value = jnp.where(lev == l, block[l * mem_dev : (l + 1) * mem_dev], value)
        gathered[me_mem, :, pl.ds(start, 128)] = value
        obs_horiz[:, pl.ds(start, 128)] = block[stack : stack + 8]
        return carry

    lax.fori_loop(0, slots // 128, sort_out, 0)
    obs_copies = [
        send(gathered.at[me_mem], gathered.at[me_mem], obs_send.at[d], obs_recv.at[d], peer)
        for d, peer in enumerate(others)
    ]
    for copy in mean_copies:
        copy.wait_recv()
    field = partial[0]
    for g in range(1, n_mem):
        field = field + partial[g]
    mean[...] = field / (n_mem * mem_dev)
    for copy in obs_copies:
        copy.wait_recv()
    obs_prior[...] = gathered[...]
    to_left.wait_send()
    to_right.wait_send()
    for copy in mean_copies + obs_copies:
        copy.wait_send()


def gram_kernel(
    n_lon, n_mem, mem_dev, norm,
    obs_prior, obs_horiz, level, vert, count, value, var,
    system,
    perts, weighted, staged, heard, whole,
    part_send, part_recv, lon_send, lon_recv, mem_send, mem_recv,
):
    slots = level.shape[1]
    layers = vert.shape[1]
    total = n_mem * mem_dev
    local = mem_dev * MODES
    size = total * MODES
    me = lax.axis_index("lon")
    me_mem = lax.axis_index("mem")
    lon_peers = axis_peers("lon", n_lon)
    mem_peers = axis_peers("mem", n_mem)

    lev = level[...]
    states = obs_prior[...].reshape(total, slots)
    centre = jnp.sum(states, axis=0, keepdims=True) / total
    slot = lax.broadcasted_iota(jnp.int32, (1, slots), 1)
    live = jnp.where(slot < count[0], 1.0, 0.0)
    inv_var = live / var[...]
    drive = inv_var * (value[...] - centre)
    scale = live * norm
    vert_obs = []
    for a in range(KV):
        v = jnp.full((1, slots), vert[a, 0])
        for l in range(1, layers):
            v = jnp.where(lev == l, vert[a, l], v)
        vert_obs.append(jnp.broadcast_to(v, (KH, slots)))
    modes = jnp.concatenate(vert_obs, axis=0) * obs_horiz[...]
    for g in range(n_mem):
        for m in range(mem_dev):
            row = (g * mem_dev + m) * MODES
            anomaly = obs_prior[g, m : m + 1, :] - centre
            perts[row : row + MODES, :] = anomaly * modes * scale
    start = pl.multiple_of(me_mem * local, local)
    mine = perts[pl.ds(start, local), :]
    weighted[...] = mine * inv_var
    gram = lax.dot_general(
        weighted[...], perts[...], (((1,), (1,)), ((), ())),
        precision=HIGHEST, preferred_element_type=jnp.float32,
    )
    side = jnp.sum(mine * drive, axis=1, keepdims=True)
    for d in range(n_lon):
        staged[d, :, 0:size] = gram[d * 8 : (d + 1) * 8]
        staged[d, :, size : size + 128] = jnp.broadcast_to(side[d * 8 : (d + 1) * 8], (8, 128))

    greet(lon_peers + mem_peers)
    parts = []
    for d, peer in enumerate(lon_peers):
        parts.append(
            send(staged.at[peer["lon"]], heard.at[me], part_send.at[d], part_recv.at[d], peer)
        )
    heard[me] = staged[me]
    for copy in parts:
        copy.wait_recv()
    block = heard[0]
    for d in range(1, n_lon):
        block = block + heard[d]
    whole[me_mem, me] = block
    spread = [
        send(whole.at[me_mem, me], whole.at[me_mem, me], lon_send.at[d], lon_recv.at[d], peer)
        for d, peer in enumerate(lon_peers)
    ]
    for copy in spread:
        copy.wait_recv()
    across = [
        send(whole.at[me_mem], whole.at[me_mem], mem_send.at[d], mem_recv.at[d], peer)
        for d, peer in enumerate(mem_peers)
    ]
    for copy in across:
        copy.wait_recv()
    system[...] = whole[...].reshape(size, size + 128)
    for copy in parts + spread + across:
        copy.wait_send()


def solve_kernel(system, weights, work):
    size, columns = system.shape
    row = lax.broadcasted_iota(jnp.int32, (size, columns), 0)
    col = lax.broadcasted_iota(jnp.int32, (size, columns), 1)
    work[...] = system[...] + jnp.where(row == col, 1.0, 0.0)
    depth = 64
    tile = (8, 128)
    sub = lax.broadcasted_iota(jnp.int32, tile, 0)
    outer = lax.broadcasted_iota(jnp.int32, (size, depth), 0)
    for top in range(0, size, depth):
        low = top // 128 * 128
        pieces = (columns - low) // 128
        panel = [
            [work[top + i * 8 : top + i * 8 + 8, low + k * 128 : low + (k + 1) * 128] for k in range(pieces)]
            for i in range(depth // 8)
        ]
        for s in range(depth // 8):
            lane = top - low + s * 8
            a = [jnp.broadcast_to(panel[s][0][:, lane + c : lane + c + 1], tile) for c in range(8)]
            rows = panel[s]
            for j in range(8):
                inv = 1.0 / jnp.broadcast_to(a[j][j : j + 1], tile)
                f = a[j]

                def reduce(x, j=j, inv=inv, f=f):
                    n = jnp.broadcast_to(x[j : j + 1], tile) * inv
                    return jnp.where(sub == j, n, x - f * n)

                for c in range(j + 1, 8):
                    a[c] = reduce(a[c])
                rows = [reduce(x) for x in rows]
            panel[s] = rows
            spread = [[jnp.broadcast_to(x[j : j + 1], tile) for x in rows] for j in range(8)]
            for d in range(1, depth // 8):
                i = (s + d) % (depth // 8)
                lead = panel[i][0]
                block = panel[i]
                for j in range(8):
                    f = jnp.broadcast_to(lead[:, lane + j : lane + j + 1], tile)
                    block = [x - f * y for x, y in zip(block, spread[j])]
                panel[i] = block
        for i in range(depth // 8):
            for k in range(pieces):
                work[top + i * 8 : top + i * 8 + 8, low + k * 128 : low + (k + 1) * 128] = panel[i][k]
        inside = (outer >= top) & (outer < top + depth)
        factor = jnp.where(inside, 0.0, work[:, top : top + depth])
        first = (top + depth) // 128 * 128
        work[:, first:columns] -= jnp.dot(
            factor, work[top : top + depth, first:columns],
            precision=HIGHEST, preferred_element_type=jnp.float32,
        )
    weights[...] = work[:, size : size + 128]


def analysis_kernel(
    n_mem, mem_dev, norm,
    weights, prior, mean, horiz, vert,
    analysis,
    partial, part_send, part_recv,
):
    layers = vert.shape[1]
    lats = mean.shape[2]
    me_mem = lax.axis_index("mem")
    peers = axis_peers("mem", n_mem)
    for l in range(layers):
        centre = mean[l]
        total = jnp.zeros_like(centre)
        for m in range(mem_dev):
            start = pl.multiple_of((me_mem * mem_dev + m) * MODES, 8)
            w = weights[pl.ds(start, MODES), :]
            mixed = vert[0, l] * w[0:KH] + vert[1, l] * w[KH : 2 * KH]
            mixed = jnp.concatenate([mixed] * (lats // 128), axis=1)
            coef = mixed[0:1] * horiz[0]
            for b in range(1, KH):
                coef = coef + mixed[b : b + 1] * horiz[b]
            total = total + coef * (prior[m * layers + l] - centre)
        partial[me_mem, l] = total
    greet(peers)
    copies = [
        send(partial.at[me_mem], partial.at[me_mem], part_send.at[d], part_recv.at[d], peer)
        for d, peer in enumerate(peers)
    ]
    for copy in copies:
        copy.wait_recv()
    field = partial[0]
    for g in range(1, n_mem):
        field = field + partial[g]
    analysis[...] = mean[...] + field * norm
    for copy in copies:
        copy.wait_send()


def params(collective=None):
    if collective is None:
        return pltpu.CompilerParams(vmem_limit_bytes=VMEM_LIMIT)
    return pltpu.CompilerParams(
        vmem_limit_bytes=VMEM_LIMIT, collective_id=collective, has_side_effects=True
    )


def fast_device(
    members, courant_lon, courant_lat, vert_modes, horiz_modes,
    obs_index, obs_count, obs_value, obs_var,
):
    f32 = jnp.float32
    mem_dev, layers, width, lats = members.shape
    n_lon = lax.axis_size("lon")
    n_mem = lax.axis_size("mem")
    total = mem_dev * n_mem
    size = total * MODES
    norm = (total - 1) ** (-0.5)
    slots = obs_index.shape[0]
    stack = mem_dev * layers
    cells = width * lats
    level = (obs_index // cells).reshape(1, slots)
    within = obs_index % cells
    dma = pltpu.SemaphoreType.DMA
    halves = lats // 128
    edge_rows = 2 * stack + 2 * layers
    prior, mean, obs_prior, obs_horiz = pl.pallas_call(
        functools.partial(advect_kernel, n_lon, n_mem, mem_dev),
        out_shape=(
            jax.ShapeDtypeStruct((stack, width, lats), f32),
            jax.ShapeDtypeStruct((layers, width, lats), f32),
            jax.ShapeDtypeStruct((n_mem, mem_dev, slots), f32),
            jax.ShapeDtypeStruct((8, slots), f32),
        ),
        in_specs=[vmem()] * 5 + [smem()],
        out_specs=(vmem(),) * 4,
        scratch_shapes=[
            pltpu.VMEM((2, edge_rows, lats), f32),
            pltpu.VMEM((2, edge_rows, lats), f32),
            pltpu.VMEM((stack, width + 8, lats), f32),
            pltpu.VMEM((layers, width + 8, lats), f32),
            pltpu.VMEM((layers, width + 8, lats), f32),
            pltpu.VMEM((n_mem, layers, width, lats), f32),
            pltpu.VMEM((halves, width * 40, 128), f32),
            pltpu.VMEM((cells, 128), f32),
            pltpu.VMEM((slots, 128), f32),
            pltpu.VMEM((n_mem, mem_dev, slots), f32),
            dma((2,)), dma((2,)),
            dma((n_mem - 1,)), dma((n_mem - 1,)),
            dma((n_mem - 1,)), dma((n_mem - 1,)),
        ],
        compiler_params=params(1),
        name="advect",
    )(members.reshape(stack, width, lats), courant_lon, courant_lat, horiz_modes, level, within)
    system = pl.pallas_call(
        functools.partial(gram_kernel, n_lon, n_mem, mem_dev, norm),
        out_shape=jax.ShapeDtypeStruct((size, size + 128), f32),
        in_specs=[vmem()] * 3 + [smem()] * 2 + [vmem()] * 2,
        out_specs=vmem(),
        scratch_shapes=[
            pltpu.VMEM((size, slots), f32),
            pltpu.VMEM((mem_dev * MODES, slots), f32),
            pltpu.VMEM((n_lon, 8, size + 128), f32),
            pltpu.VMEM((n_lon, 8, size + 128), f32),
            pltpu.VMEM((n_mem, n_lon, 8, size + 128), f32),
            dma((n_lon - 1,)), dma((n_lon - 1,)),
            dma((n_lon - 1,)), dma((n_lon - 1,)),
            dma((n_mem - 1,)), dma((n_mem - 1,)),
        ],
        compiler_params=params(2),
        name="gram",
    )(
        obs_prior, obs_horiz, level, vert_modes, obs_count,
        obs_value.reshape(1, slots), obs_var.reshape(1, slots),
    )
    weights = pl.pallas_call(
        solve_kernel,
        out_shape=jax.ShapeDtypeStruct((size, 128), f32),
        in_specs=[vmem()],
        out_specs=vmem(),
        scratch_shapes=[pltpu.VMEM((size, size + 128), f32)],
        compiler_params=params(),
        name="solve",
    )(system)
    analysis = pl.pallas_call(
        functools.partial(analysis_kernel, n_mem, mem_dev, norm),
        out_shape=jax.ShapeDtypeStruct((layers, width, lats), f32),
        in_specs=[vmem()] * 4 + [smem()],
        out_specs=vmem(),
        scratch_shapes=[
            pltpu.VMEM((n_mem, layers, width, lats), f32),
            dma((n_mem - 1,)), dma((n_mem - 1,)),
        ],
        compiler_params=params(3),
        name="analysis",
    )(weights, prior, mean, horiz_modes, vert_modes)
    return prior.reshape(members.shape), analysis


def padded(block, sides, width):
    for axis, dim in sides:
        count = lax.axis_size(axis)
        forward = [(i, i + 1) for i in range(count - 1)]
        forward.append((count - 1, 0))
        backward = [(target, source) for source, target in forward]
        low = lax.ppermute(
            lax.slice_in_dim(block, block.shape[dim] - width, None, axis=dim), axis, forward
        )
        high = lax.ppermute(lax.slice_in_dim(block, 0, width, axis=dim), axis, backward)
        block = jnp.concatenate([low, block, high], axis=dim)
    return block


def update(centre, western, eastern, flow_lon, flow_lat):
    zero_col = jnp.zeros_like(centre[..., :1])
    south_boundary = jnp.concatenate([zero_col, centre[..., :-1]], axis=-1)
    northern = jnp.concatenate([centre[..., 1:], zero_col], axis=-1)
    result = centre - jnp.maximum(flow_lon, 0.0) * (centre - western)
    result = result - jnp.minimum(flow_lon, 0.0) * (eastern - centre)
    result = result - jnp.maximum(flow_lat, 0.0) * (centre - south_boundary)
    result = result - jnp.minimum(flow_lat, 0.0) * (northern - centre)
    return result


def per_device(
    members,
    courant_lon,
    courant_lat,
    vert_modes,
    horiz_modes,
    obs_index,
    obs_count,
    obs_value,
    obs_var,
):
    mem_dev, layer_tally, band_width, lat_rows = members.shape
    sample_tally_overall = mem_dev * lax.axis_size("mem")
    rim_depth = ADV_STEPS
    stacked = jnp.concatenate(
        [members.reshape(mem_dev * layer_tally, band_width, lat_rows), courant_lon, courant_lat],
        axis=0,
    )
    extended = padded(stacked, (("lon", 1),), rim_depth)
    split_at = mem_dev * layer_tally
    prognostic_vector = extended[:split_at].reshape(
        mem_dev, layer_tally, band_width + 2 * rim_depth, lat_rows
    )
    flow_lon_ext = extended[split_at : split_at + layer_tally]
    meridional_wind_padded = extended[split_at + layer_tally :]
    for section in range(rim_depth):
        out_cols = band_width + 2 * (rim_depth - 1 - section)
        first_col = section + 1
        prognostic_vector = update(
            prognostic_vector[:, :, 1 : out_cols + 1],
            prognostic_vector[:, :, 0:out_cols],
            prognostic_vector[:, :, 2 : out_cols + 2],
            flow_lon_ext[:, first_col : first_col + out_cols],
            meridional_wind_padded[:, first_col : first_col + out_cols],
        )
    sample_centroid = lax.psum(jnp.sum(prognostic_vector, axis=0), "mem") / sample_tally_overall
    sample_departure = prognostic_vector - sample_centroid[None]
    norm_scale = (sample_tally_overall - 1) ** (-0.5)
    obs_slots = obs_index.shape[0]
    band_cells = band_width * lat_rows
    level_idx = obs_index // band_cells
    within = obs_index % band_cells
    anomaly_obs = jnp.take(sample_departure.reshape(mem_dev, -1), obs_index, axis=1)
    mean_obs = jnp.take(sample_centroid.reshape(-1), obs_index)
    vert_obs = jnp.take(vert_modes, level_idx, axis=1)
    horiz_obs = jnp.take(horiz_modes.reshape(KH, -1), within, axis=1)
    modes_obs = (vert_obs[:, None, :] * horiz_obs[None, :, :]).reshape(KV * KH, obs_slots)
    live_mask = (jnp.arange(obs_slots, dtype=jnp.int32) < obs_count[0]).astype(jnp.float32)
    obs_perts = (
        anomaly_obs[:, None, :] * modes_obs[None, :, :] * (live_mask * norm_scale)[None, None, :]
    )
    obs_perts = obs_perts.reshape(mem_dev * KV * KH, obs_slots)
    inv_var = live_mask / obs_var
    innovation = obs_value - mean_obs
    all_perts = lax.all_gather(obs_perts, "mem", axis=0, tiled=True)
    gram_part = jnp.dot(all_perts * inv_var[None, :], all_perts.T, precision=lax.Precision.HIGHEST)
    side_part = jnp.dot(all_perts, inv_var * innovation, precision=lax.Precision.HIGHEST)
    gram_matrix, right_side = lax.psum((gram_part, side_part), "lon")
    system = jnp.eye(gram_matrix.shape[0], dtype=jnp.float32) + gram_matrix
    factor = jnp.linalg.cholesky(system)
    weights = jax.scipy.linalg.cho_solve((factor, True), right_side)
    w_mat = weights.reshape(sample_tally_overall, KV * KH)
    w_local = lax.dynamic_slice_in_dim(w_mat, lax.axis_index("mem") * mem_dev, mem_dev, 0)
    mode_coef = jnp.einsum(
        "mk,mlij->klij", w_local, sample_departure, precision=lax.Precision.HIGHEST
    )
    mode_coef = mode_coef.reshape(KV, KH, layer_tally, band_width, lat_rows)
    inc_part = (
        jnp.einsum(
            "al,bij,ablij->lij", vert_modes, horiz_modes, mode_coef, precision=lax.Precision.HIGHEST
        )
        * norm_scale
    )
    posterior_adjustment = lax.psum(inc_part, "mem")
    return (prognostic_vector, sample_centroid + posterior_adjustment)


def choose(*args):
    mem_dev, layers, width, lats = args[0].shape
    n_lon = lax.axis_size("lon")
    fits = (
        mem_dev == 8
        and layers == 4
        and width % 8 == 0
        and lats % 128 == 0
        and args[5].shape[0] % 128 == 0
        and n_lon > 2
        and mem_dev * MODES == 8 * n_lon
        and (mem_dev * lax.axis_size("mem") * MODES) % 128 == 0
    )
    return fast_device(*args) if fits else per_device(*args)


def solution(mesh):
    placed = (
        P("mem", None, "lon", None),
        P(None, "lon", None),
        P(None, "lon", None),
        P(),
        P(None, "lon", None),
        P("lon"),
        P("lon"),
        P("lon"),
        P("lon"),
    )
    return jax.shard_map(
        choose,
        mesh=mesh,
        in_specs=placed,
        out_specs=(P("mem", None, "lon", None), P(None, "lon", None)),
        check_vma=False,
    )
```

```python
import functools

import jax
import jax.numpy as jnp
from jax import lax
from jax.experimental import pallas as pl
from jax.experimental.pallas import tpu as pltpu
from jax.sharding import PartitionSpec as P

KV = 2
KH = 4
ADV_STEPS = 2
MODES = KV * KH
MESH = pl.DeviceIdType.MESH
VMEM_LIMIT = 56 * 1024 * 1024
HIGHEST = lax.Precision.HIGHEST


def vmem():
    return pl.BlockSpec(memory_space=pltpu.VMEM)


def smem():
    return pl.BlockSpec(memory_space=pltpu.SMEM)


def greet(peers):
    barrier = pltpu.get_barrier_semaphore()
    for peer in peers:
        pl.semaphore_signal(barrier, inc=1, device_id=peer, device_id_type=MESH)
    return barrier


def axis_peers(axis, count):
    me = lax.axis_index(axis)
    return [{axis: lax.rem(me + d, count)} for d in range(1, count)]


def send(src, dst, send_sem, recv_sem, peer):
    copy = pltpu.make_async_remote_copy(
        src_ref=src, dst_ref=dst, send_sem=send_sem, recv_sem=recv_sem,
        device_id=peer, device_id_type=MESH,
    )
    copy.start()
    return copy


def advect_kernel(
    n_lon, n_mem, mem_dev,
    members, cx, cy, horiz, level, within,
    prior, mean, obs_prior, obs_horiz,
    edge_out, edge_in, ext, cx_ext, cy_ext, partial, cols, table, picked, gathered,
    edge_send, edge_recv, mean_send, mean_recv, obs_send, obs_recv,
):
    layers = cx.shape[0]
    stack, width, lats = members.shape
    rows = 40
    halves = lats // 128
    me = lax.axis_index("lon")
    me_mem = lax.axis_index("mem")
    left = {"lon": lax.rem(me + n_lon - 1, n_lon)}
    right = {"lon": lax.rem(me + 1, n_lon)}
    others = axis_peers("mem", n_mem)

    barrier = greet([left, right] + others)
    for side, (first, second, rim) in enumerate(((0, 1, 0), (width - 2, width - 1, width - 1))):
        edge_out[side, 0:stack, :] = members[:, first, :]
        edge_out[side, stack : 2 * stack, :] = members[:, second, :]
        edge_out[side, 2 * stack : 2 * stack + layers, :] = cx[:, rim, :]
        edge_out[side, 2 * stack + layers : 2 * stack + 2 * layers, :] = cy[:, rim, :]
    pl.semaphore_wait(barrier, 2 + len(others))
    to_left = send(edge_out.at[0], edge_in.at[1], edge_send.at[0], edge_recv.at[1], left)
    to_right = send(edge_out.at[1], edge_in.at[0], edge_send.at[1], edge_recv.at[0], right)

    ext[:, 4 : 4 + width, :] = members[...]
    cx_ext[:, 4 : 4 + width, :] = cx[...]
    cy_ext[:, 4 : 4 + width, :] = cy[...]
    for b in range(2 * KH):
        for h in range(halves):
            cols[h, pl.ds(stack + b, width, stride=rows), :] = horiz[
                b % KH, :, h * 128 : (h + 1) * 128
            ]
    to_left.wait_recv()
    to_right.wait_recv()
    high = 4 + width
    ext[:, 2, :] = edge_in[0, 0:stack, :]
    ext[:, 3, :] = edge_in[0, stack : 2 * stack, :]
    ext[:, high, :] = edge_in[1, 0:stack, :]
    ext[:, high + 1, :] = edge_in[1, stack : 2 * stack, :]
    for side, row in ((0, 3), (1, high)):
        cx_ext[:, row, :] = edge_in[side, 2 * stack : 2 * stack + layers, :]
        cy_ext[:, row, :] = edge_in[side, 2 * stack + layers : 2 * stack + 2 * layers, :]

    ext_rows = width + 8
    lane = lax.broadcasted_iota(jnp.int32, (ext_rows, lats), 1)
    for l in range(layers):
        cx_l = cx_ext[l]
        cy_l = cy_ext[l]
        east_flow = jnp.maximum(cx_l, 0.0)
        west_flow = jnp.minimum(cx_l, 0.0)
        north_flow = jnp.maximum(cy_l, 0.0)
        south_flow = jnp.minimum(cy_l, 0.0)

        def step(m, total, l=l, flows=(east_flow, west_flow, north_flow, south_flow)):
            q = ext[m * layers + l]
            for _ in range(ADV_STEPS):
                qw = pltpu.roll(q, 1, 0)
                qe = pltpu.roll(q, ext_rows - 1, 0)
                qs = jnp.where(lane == 0, 0.0, pltpu.roll(q, 1, 1))
                qn = jnp.where(lane == lats - 1, 0.0, pltpu.roll(q, lats - 1, 1))
                r = q - flows[0] * (q - qw)
                r = r - flows[1] * (qe - q)
                r = r - flows[2] * (q - qs)
                q = r - flows[3] * (qn - q)
            inner = q[4 : 4 + width, :]
            prior[m * layers + l] = inner
            for h in range(halves):
                cols[h, pl.ds(l * mem_dev + m, width, stride=rows), :] = inner[
                    :, h * 128 : (h + 1) * 128
                ]
            return total + inner

        total = lax.fori_loop(
            0, mem_dev, step, jnp.zeros((width, lats), jnp.float32), unroll=2
        )
        partial[me_mem, l] = total

    mean_copies = [
        send(partial.at[me_mem], partial.at[me_mem], mean_send.at[d], mean_recv.at[d], peer)
        for d, peer in enumerate(others)
    ]

    def turn(g, carry):
        for u in range(4):
            i = g * 4 + u
            blocks = [cols[h, pl.ds(pl.multiple_of(i * rows, 8), rows), :].T for h in range(halves)]
            for h in range(halves):
                table[pl.ds(pl.multiple_of(i * lats + h * 128, 128), 128), 0:rows] = blocks[h]
        return carry

    lax.fori_loop(0, width // 4, turn, 0)

    slots = within.shape[0]
    unroll = 32
    chunks = obs_send.shape[0]
    chunk = slots // chunks

    def fetch(g, carry):
        found = [table[pl.ds(within[g * unroll + u], 1), :] for u in range(unroll)]
        for u in range(unroll):
            picked[pl.ds(g * unroll + u, 1), :] = found[u]
        return carry

    def sort_out(c, carry):
        start = pl.multiple_of(c * 128, 128)
        block = picked[pl.ds(start, 128), :].T
        lev = level[:, pl.ds(start, 128)]
        value = block[0:mem_dev]
        for l in range(1, layers):
            value = jnp.where(lev == l, block[l * mem_dev : (l + 1) * mem_dev], value)
        gathered[me_mem, :, pl.ds(start, 128)] = value
        obs_horiz[:, pl.ds(start, 128)] = block[stack : stack + 8]
        return carry

    obs_copies = []
    for c in range(chunks):
        lax.fori_loop(c * chunk // unroll, (c + 1) * chunk // unroll, fetch, 0)
        lax.fori_loop(c * chunk // 128, (c + 1) * chunk // 128, sort_out, 0, unroll=True)
        piece = gathered.at[me_mem, :, pl.ds(c * chunk, chunk)]
        for d, peer in enumerate(others):
            obs_copies.append(send(piece, piece, obs_send.at[c, d], obs_recv.at[c, d], peer))
    for copy in mean_copies:
        copy.wait_recv()
    field = partial[0]
    for g in range(1, n_mem):
        field = field + partial[g]
    mean[...] = field / (n_mem * mem_dev)
    for copy in obs_copies:
        copy.wait_recv()
    obs_prior[...] = gathered[...]
    to_left.wait_send()
    to_right.wait_send()
    for copy in mean_copies + obs_copies:
        copy.wait_send()


def gram_kernel(
    n_lon, n_mem, mem_dev, norm,
    obs_prior, obs_horiz, level, vert, count, value, var,
    system,
    perts, weighted, staged, heard, whole,
    part_send, part_recv, lon_send, lon_recv, mem_send, mem_recv,
):
    slots = level.shape[1]
    layers = vert.shape[1]
    total = n_mem * mem_dev
    local = mem_dev * MODES
    size = total * MODES
    me = lax.axis_index("lon")
    me_mem = lax.axis_index("mem")
    lon_peers = axis_peers("lon", n_lon)
    mem_peers = axis_peers("mem", n_mem)

    barrier = greet(lon_peers + mem_peers)
    lev = level[...]
    states = obs_prior[...].reshape(total, slots)
    centre = jnp.sum(states, axis=0, keepdims=True) / total
    slot = lax.broadcasted_iota(jnp.int32, (1, slots), 1)
    live = jnp.where(slot < count[0], 1.0, 0.0)
    inv_var = live / var[...]
    drive = inv_var * (value[...] - centre)
    scale = live * norm
    vert_obs = []
    for a in range(KV):
        v = jnp.full((1, slots), vert[a, 0])
        for l in range(1, layers):
            v = jnp.where(lev == l, vert[a, l], v)
        vert_obs.append(jnp.broadcast_to(v, (KH, slots)))
    modes = jnp.concatenate(vert_obs, axis=0) * obs_horiz[...]
    for g in range(n_mem):
        for m in range(mem_dev):
            row = (g * mem_dev + m) * MODES
            anomaly = obs_prior[g, m : m + 1, :] - centre
            perts[row : row + MODES, :] = anomaly * modes * scale
    start = pl.multiple_of(me_mem * local, local)
    mine = perts[pl.ds(start, local), :]
    weighted[...] = mine * inv_var
    gram = lax.dot_general(
        weighted[...], perts[...], (((1,), (1,)), ((), ())),
        precision=HIGHEST, preferred_element_type=jnp.float32,
    )
    side = jnp.sum(mine * drive, axis=1, keepdims=True)
    for d in range(n_lon):
        staged[d, :, 0:size] = gram[d * 8 : (d + 1) * 8]
        staged[d, :, size : size + 128] = jnp.broadcast_to(side[d * 8 : (d + 1) * 8], (8, 128))

    pl.semaphore_wait(barrier, len(lon_peers) + len(mem_peers))
    parts = []
    for d, peer in enumerate(lon_peers):
        parts.append(
            send(staged.at[peer["lon"]], heard.at[me], part_send.at[d], part_recv.at[d], peer)
        )
    heard[me] = staged[me]
    for copy in parts:
        copy.wait_recv()
    block = heard[0]
    for d in range(1, n_lon):
        block = block + heard[d]
    whole[me_mem, me] = block
    spread = [
        send(whole.at[me_mem, me], whole.at[me_mem, me], lon_send.at[d], lon_recv.at[d], peer)
        for d, peer in enumerate(lon_peers)
    ]
    for copy in spread:
        copy.wait_recv()
    across = [
        send(whole.at[me_mem], whole.at[me_mem], mem_send.at[d], mem_recv.at[d], peer)
        for d, peer in enumerate(mem_peers)
    ]
    for copy in across:
        copy.wait_recv()
    system[...] = whole[...].reshape(size, size + 128)
    for copy in parts + spread + across:
        copy.wait_send()


def solve_kernel(system, prior, weights, prior_out, work, copy_sem):
    size, columns = system.shape
    keep = pltpu.make_async_copy(prior, prior_out, copy_sem)
    keep.start()
    row = lax.broadcasted_iota(jnp.int32, (size, columns), 0)
    col = lax.broadcasted_iota(jnp.int32, (size, columns), 1)
    work[...] = system[...] + jnp.where(row == col, 1.0, 0.0)
    depth = 64
    tile = (8, 128)
    sub = lax.broadcasted_iota(jnp.int32, tile, 0)
    outer = lax.broadcasted_iota(jnp.int32, (size, depth), 0)
    for top in range(0, size, depth):
        low = top // 128 * 128
        pieces = (columns - low) // 128
        panel = [
            [work[top + i * 8 : top + i * 8 + 8, low + k * 128 : low + (k + 1) * 128] for k in range(pieces)]
            for i in range(depth // 8)
        ]
        for s in range(depth // 8):
            lane = top - low + s * 8
            a = [jnp.broadcast_to(panel[s][0][:, lane + c : lane + c + 1], tile) for c in range(8)]
            rows = panel[s]
            for j in range(8):
                inv = 1.0 / jnp.broadcast_to(a[j][j : j + 1], tile)
                f = a[j]

                def reduce(x, j=j, inv=inv, f=f):
                    n = jnp.broadcast_to(x[j : j + 1], tile) * inv
                    return jnp.where(sub == j, n, x - f * n)

                for c in range(j + 1, 8):
                    a[c] = reduce(a[c])
                rows = [reduce(x) for x in rows]
            panel[s] = rows
            spread = [[jnp.broadcast_to(x[j : j + 1], tile) for x in rows] for j in range(8)]
            for d in range(1, depth // 8):
                i = (s + d) % (depth // 8)
                lead = panel[i][0]
                block = panel[i]
                for j in range(8):
                    f = jnp.broadcast_to(lead[:, lane + j : lane + j + 1], tile)
                    block = [x - f * y for x, y in zip(block, spread[j])]
                panel[i] = block
        for i in range(depth // 8):
            for k in range(pieces):
                work[top + i * 8 : top + i * 8 + 8, low + k * 128 : low + (k + 1) * 128] = panel[i][k]
        inside = (outer >= top) & (outer < top + depth)
        factor = jnp.where(inside, 0.0, work[:, top : top + depth])
        first = (top + depth) // 128 * 128
        work[:, first:columns] -= jnp.dot(
            factor, work[top : top + depth, first:columns],
            precision=HIGHEST, preferred_element_type=jnp.float32,
        )
    weights[...] = work[:, size : size + 128]
    keep.wait()


def analysis_kernel(
    n_mem, mem_dev, norm,
    weights, prior, mean, horiz, vert,
    analysis,
    partial, part_send, part_recv,
):
    layers = vert.shape[1]
    lats = mean.shape[2]
    me_mem = lax.axis_index("mem")
    peers = axis_peers("mem", n_mem)
    barrier = greet(peers)
    copies = []
    for l in range(layers):
        centre = mean[l]
        total = jnp.zeros_like(centre)
        for m in range(mem_dev):
            start = pl.multiple_of((me_mem * mem_dev + m) * MODES, 8)
            w = weights[pl.ds(start, MODES), :]
            mixed = vert[0, l] * w[0:KH] + vert[1, l] * w[KH : 2 * KH]
            mixed = jnp.concatenate([mixed] * (lats // 128), axis=1)
            coef = mixed[0:1] * horiz[0]
            for b in range(1, KH):
                coef = coef + mixed[b : b + 1] * horiz[b]
            total = total + coef * (prior[m * layers + l] - centre)
        partial[me_mem, l] = total
        if l == 0:
            pl.semaphore_wait(barrier, len(peers))
        piece = partial.at[me_mem, l]
        for d, peer in enumerate(peers):
            copies.append(send(piece, piece, part_send.at[l, d], part_recv.at[l, d], peer))
    for l in range(layers):
        for copy in copies[l * len(peers) : (l + 1) * len(peers)]:
            copy.wait_recv()
        field = partial[0, l]
        for g in range(1, n_mem):
            field = field + partial[g, l]
        analysis[l] = mean[l] + field * norm
    for copy in copies:
        copy.wait_send()


def params(collective=None):
    if collective is None:
        return pltpu.CompilerParams(vmem_limit_bytes=VMEM_LIMIT)
    return pltpu.CompilerParams(
        vmem_limit_bytes=VMEM_LIMIT, collective_id=collective, has_side_effects=True
    )


def fast_device(
    members, courant_lon, courant_lat, vert_modes, horiz_modes,
    obs_index, obs_count, obs_value, obs_var,
):
    f32 = jnp.float32
    mem_dev, layers, width, lats = members.shape
    n_lon = lax.axis_size("lon")
    n_mem = lax.axis_size("mem")
    total = mem_dev * n_mem
    size = total * MODES
    norm = (total - 1) ** (-0.5)
    slots = obs_index.shape[0]
    stack = mem_dev * layers
    cells = width * lats
    level = sum((obs_index >= l * cells).astype(jnp.int32) for l in range(1, layers))
    within = obs_index - cells * level
    level = level.reshape(1, slots)
    dma = pltpu.SemaphoreType.DMA
    halves = lats // 128
    edge_rows = 2 * stack + 2 * layers
    prior, mean, obs_prior, obs_horiz = pl.pallas_call(
        functools.partial(advect_kernel, n_lon, n_mem, mem_dev),
        out_shape=(
            jax.ShapeDtypeStruct((stack, width, lats), f32),
            jax.ShapeDtypeStruct((layers, width, lats), f32),
            jax.ShapeDtypeStruct((n_mem, mem_dev, slots), f32),
            jax.ShapeDtypeStruct((8, slots), f32),
        ),
        in_specs=[vmem()] * 5 + [smem()],
        out_specs=(vmem(),) * 4,
        scratch_shapes=[
            pltpu.VMEM((2, edge_rows, lats), f32),
            pltpu.VMEM((2, edge_rows, lats), f32),
            pltpu.VMEM((stack, width + 8, lats), f32),
            pltpu.VMEM((layers, width + 8, lats), f32),
            pltpu.VMEM((layers, width + 8, lats), f32),
            pltpu.VMEM((n_mem, layers, width, lats), f32),
            pltpu.VMEM((halves, width * 40, 128), f32),
            pltpu.VMEM((cells, 128), f32),
            pltpu.VMEM((slots, 128), f32),
            pltpu.VMEM((n_mem, mem_dev, slots), f32),
            dma((2,)), dma((2,)),
            dma((n_mem - 1,)), dma((n_mem - 1,)),
            dma((4, n_mem - 1)), dma((4, n_mem - 1)),
        ],
        compiler_params=params(1),
        name="advect",
    )(members.reshape(stack, width, lats), courant_lon, courant_lat, horiz_modes, level, within)
    system = pl.pallas_call(
        functools.partial(gram_kernel, n_lon, n_mem, mem_dev, norm),
        out_shape=jax.ShapeDtypeStruct((size, size + 128), f32),
        in_specs=[vmem()] * 3 + [smem()] * 2 + [vmem()] * 2,
        out_specs=vmem(),
        scratch_shapes=[
            pltpu.VMEM((size, slots), f32),
            pltpu.VMEM((mem_dev * MODES, slots), f32),
            pltpu.VMEM((n_lon, 8, size + 128), f32),
            pltpu.VMEM((n_lon, 8, size + 128), f32),
            pltpu.VMEM((n_mem, n_lon, 8, size + 128), f32),
            dma((n_lon - 1,)), dma((n_lon - 1,)),
            dma((n_lon - 1,)), dma((n_lon - 1,)),
            dma((n_mem - 1,)), dma((n_mem - 1,)),
        ],
        compiler_params=params(2),
        name="gram",
    )(
        obs_prior, obs_horiz, level, vert_modes, obs_count,
        obs_value.reshape(1, slots), obs_var.reshape(1, slots),
    )
    anywhere = pl.BlockSpec(memory_space=pl.ANY)
    weights, prior_out = pl.pallas_call(
        solve_kernel,
        out_shape=(
            jax.ShapeDtypeStruct((size, 128), f32),
            jax.ShapeDtypeStruct(prior.shape, f32),
        ),
        in_specs=[vmem(), vmem()],
        out_specs=(vmem(), anywhere),
        scratch_shapes=[pltpu.VMEM((size, size + 128), f32), dma],
        compiler_params=params(),
        name="solve",
    )(system, prior)
    analysis = pl.pallas_call(
        functools.partial(analysis_kernel, n_mem, mem_dev, norm),
        out_shape=jax.ShapeDtypeStruct((layers, width, lats), f32),
        in_specs=[vmem()] * 4 + [smem()],
        out_specs=vmem(),
        scratch_shapes=[
            pltpu.VMEM((n_mem, layers, width, lats), f32),
            dma((layers, n_mem - 1)), dma((layers, n_mem - 1)),
        ],
        compiler_params=params(3),
        name="analysis",
    )(weights, prior, mean, horiz_modes, vert_modes)
    return prior_out.reshape(members.shape), analysis


def padded(block, sides, width):
    for axis, dim in sides:
        count = lax.axis_size(axis)
        forward = [(i, i + 1) for i in range(count - 1)]
        forward.append((count - 1, 0))
        backward = [(target, source) for source, target in forward]
        low = lax.ppermute(
            lax.slice_in_dim(block, block.shape[dim] - width, None, axis=dim), axis, forward
        )
        high = lax.ppermute(lax.slice_in_dim(block, 0, width, axis=dim), axis, backward)
        block = jnp.concatenate([low, block, high], axis=dim)
    return block


def update(centre, western, eastern, flow_lon, flow_lat):
    zero_col = jnp.zeros_like(centre[..., :1])
    south_boundary = jnp.concatenate([zero_col, centre[..., :-1]], axis=-1)
    northern = jnp.concatenate([centre[..., 1:], zero_col], axis=-1)
    result = centre - jnp.maximum(flow_lon, 0.0) * (centre - western)
    result = result - jnp.minimum(flow_lon, 0.0) * (eastern - centre)
    result = result - jnp.maximum(flow_lat, 0.0) * (centre - south_boundary)
    result = result - jnp.minimum(flow_lat, 0.0) * (northern - centre)
    return result


def per_device(
    members,
    courant_lon,
    courant_lat,
    vert_modes,
    horiz_modes,
    obs_index,
    obs_count,
    obs_value,
    obs_var,
):
    mem_dev, layer_tally, band_width, lat_rows = members.shape
    sample_tally_overall = mem_dev * lax.axis_size("mem")
    rim_depth = ADV_STEPS
    stacked = jnp.concatenate(
        [members.reshape(mem_dev * layer_tally, band_width, lat_rows), courant_lon, courant_lat],
        axis=0,
    )
    extended = padded(stacked, (("lon", 1),), rim_depth)
    split_at = mem_dev * layer_tally
    prognostic_vector = extended[:split_at].reshape(
        mem_dev, layer_tally, band_width + 2 * rim_depth, lat_rows
    )
    flow_lon_ext = extended[split_at : split_at + layer_tally]
    meridional_wind_padded = extended[split_at + layer_tally :]
    for section in range(rim_depth):
        out_cols = band_width + 2 * (rim_depth - 1 - section)
        first_col = section + 1
        prognostic_vector = update(
            prognostic_vector[:, :, 1 : out_cols + 1],
            prognostic_vector[:, :, 0:out_cols],
            prognostic_vector[:, :, 2 : out_cols + 2],
            flow_lon_ext[:, first_col : first_col + out_cols],
            meridional_wind_padded[:, first_col : first_col + out_cols],
        )
    sample_centroid = lax.psum(jnp.sum(prognostic_vector, axis=0), "mem") / sample_tally_overall
    sample_departure = prognostic_vector - sample_centroid[None]
    norm_scale = (sample_tally_overall - 1) ** (-0.5)
    obs_slots = obs_index.shape[0]
    band_cells = band_width * lat_rows
    level_idx = obs_index // band_cells
    within = obs_index % band_cells
    anomaly_obs = jnp.take(sample_departure.reshape(mem_dev, -1), obs_index, axis=1)
    mean_obs = jnp.take(sample_centroid.reshape(-1), obs_index)
    vert_obs = jnp.take(vert_modes, level_idx, axis=1)
    horiz_obs = jnp.take(horiz_modes.reshape(KH, -1), within, axis=1)
    modes_obs = (vert_obs[:, None, :] * horiz_obs[None, :, :]).reshape(KV * KH, obs_slots)
    live_mask = (jnp.arange(obs_slots, dtype=jnp.int32) < obs_count[0]).astype(jnp.float32)
    obs_perts = (
        anomaly_obs[:, None, :] * modes_obs[None, :, :] * (live_mask * norm_scale)[None, None, :]
    )
    obs_perts = obs_perts.reshape(mem_dev * KV * KH, obs_slots)
    inv_var = live_mask / obs_var
    innovation = obs_value - mean_obs
    all_perts = lax.all_gather(obs_perts, "mem", axis=0, tiled=True)
    gram_part = jnp.dot(all_perts * inv_var[None, :], all_perts.T, precision=lax.Precision.HIGHEST)
    side_part = jnp.dot(all_perts, inv_var * innovation, precision=lax.Precision.HIGHEST)
    gram_matrix, right_side = lax.psum((gram_part, side_part), "lon")
    system = jnp.eye(gram_matrix.shape[0], dtype=jnp.float32) + gram_matrix
    factor = jnp.linalg.cholesky(system)
    weights = jax.scipy.linalg.cho_solve((factor, True), right_side)
    w_mat = weights.reshape(sample_tally_overall, KV * KH)
    w_local = lax.dynamic_slice_in_dim(w_mat, lax.axis_index("mem") * mem_dev, mem_dev, 0)
    mode_coef = jnp.einsum(
        "mk,mlij->klij", w_local, sample_departure, precision=lax.Precision.HIGHEST
    )
    mode_coef = mode_coef.reshape(KV, KH, layer_tally, band_width, lat_rows)
    inc_part = (
        jnp.einsum(
            "al,bij,ablij->lij", vert_modes, horiz_modes, mode_coef, precision=lax.Precision.HIGHEST
        )
        * norm_scale
    )
    posterior_adjustment = lax.psum(inc_part, "mem")
    return (prognostic_vector, sample_centroid + posterior_adjustment)


def choose(*args):
    mem_dev, layers, width, lats = args[0].shape
    n_lon = lax.axis_size("lon")
    fits = (
        mem_dev == 8
        and layers == 4
        and width % 8 == 0
        and lats % 128 == 0
        and args[5].shape[0] % 512 == 0
        and n_lon > 2
        and mem_dev * MODES == 8 * n_lon
        and (mem_dev * lax.axis_size("mem") * MODES) % 128 == 0
    )
    return fast_device(*args) if fits else per_device(*args)


def solution(mesh):
    placed = (
        P("mem", None, "lon", None),
        P(None, "lon", None),
        P(None, "lon", None),
        P(),
        P(None, "lon", None),
        P("lon"),
        P("lon"),
        P("lon"),
        P("lon"),
    )
    return jax.shard_map(
        choose,
        mesh=mesh,
        in_specs=placed,
        out_specs=(P("mem", None, "lon", None), P(None, "lon", None)),
        check_vma=False,
    )
```

```python
import functools

import jax
import jax.numpy as jnp
from jax import lax
from jax.experimental import pallas as pl
from jax.experimental.pallas import tpu as pltpu
from jax.sharding import PartitionSpec as P

KV = 2
KH = 4
ADV_STEPS = 2
MODES = KV * KH
MESH = pl.DeviceIdType.MESH
VMEM_LIMIT = 20 * 1024 * 1024
HIGHEST = lax.Precision.HIGHEST


def vmem():
    return pl.BlockSpec(memory_space=pltpu.VMEM)


def smem():
    return pl.BlockSpec(memory_space=pltpu.SMEM)


def greet(peers):
    barrier = pltpu.get_barrier_semaphore()
    for peer in peers:
        pl.semaphore_signal(barrier, inc=1, device_id=peer, device_id_type=MESH)
    return barrier


def axis_peers(axis, count):
    me = lax.axis_index(axis)
    return [{axis: lax.rem(me + d, count)} for d in range(1, count)]


def send(src, dst, send_sem, recv_sem, peer):
    copy = pltpu.make_async_remote_copy(
        src_ref=src, dst_ref=dst, send_sem=send_sem, recv_sem=recv_sem,
        device_id=peer, device_id_type=MESH,
    )
    copy.start()
    return copy


def advect_kernel(
    n_lon, n_mem, mem_dev,
    members, cx, cy, horiz, level, within,
    prior, mean, obs_prior, obs_horiz,
    edge_out, edge_in, ext, cx_ext, cy_ext, partial, cols, table, picked, gathered,
    edge_send, edge_recv, mean_send, mean_recv, obs_send, obs_recv,
):
    layers = cx.shape[0]
    stack, width, lats = members.shape
    rows = 40
    halves = lats // 128
    me = lax.axis_index("lon")
    me_mem = lax.axis_index("mem")
    left = {"lon": lax.rem(me + n_lon - 1, n_lon)}
    right = {"lon": lax.rem(me + 1, n_lon)}
    others = axis_peers("mem", n_mem)

    barrier = greet([left, right] + others)
    for side, (first, second, rim) in enumerate(((0, 1, 0), (width - 2, width - 1, width - 1))):
        edge_out[side, 0:stack, :] = members[:, first, :]
        edge_out[side, stack : 2 * stack, :] = members[:, second, :]
        edge_out[side, 2 * stack : 2 * stack + layers, :] = cx[:, rim, :]
        edge_out[side, 2 * stack + layers : 2 * stack + 2 * layers, :] = cy[:, rim, :]
    pl.semaphore_wait(barrier, 2 + len(others))
    to_left = send(edge_out.at[0], edge_in.at[1], edge_send.at[0], edge_recv.at[1], left)
    to_right = send(edge_out.at[1], edge_in.at[0], edge_send.at[1], edge_recv.at[0], right)

    ext[:, 4 : 4 + width, :] = members[...]
    cx_ext[:, 4 : 4 + width, :] = cx[...]
    cy_ext[:, 4 : 4 + width, :] = cy[...]
    for b in range(2 * KH):
        for h in range(halves):
            cols[h, pl.ds(stack + b, width, stride=rows), :] = horiz[
                b % KH, :, h * 128 : (h + 1) * 128
            ]
    to_left.wait_recv()
    to_right.wait_recv()
    high = 4 + width
    ext[:, 2, :] = edge_in[0, 0:stack, :]
    ext[:, 3, :] = edge_in[0, stack : 2 * stack, :]
    ext[:, high, :] = edge_in[1, 0:stack, :]
    ext[:, high + 1, :] = edge_in[1, stack : 2 * stack, :]
    for side, row in ((0, 3), (1, high)):
        cx_ext[:, row, :] = edge_in[side, 2 * stack : 2 * stack + layers, :]
        cy_ext[:, row, :] = edge_in[side, 2 * stack + layers : 2 * stack + 2 * layers, :]

    ext_rows = width + 8
    lane = lax.broadcasted_iota(jnp.int32, (ext_rows, lats), 1)
    for l in range(layers):
        cx_l = cx_ext[l]
        cy_l = cy_ext[l]
        east_flow = jnp.maximum(cx_l, 0.0)
        west_flow = jnp.minimum(cx_l, 0.0)
        north_flow = jnp.maximum(cy_l, 0.0)
        south_flow = jnp.minimum(cy_l, 0.0)

        def step(m, total, l=l, flows=(east_flow, west_flow, north_flow, south_flow)):
            q = ext[m * layers + l]
            for _ in range(ADV_STEPS):
                qw = pltpu.roll(q, 1, 0)
                qe = pltpu.roll(q, ext_rows - 1, 0)
                qs = jnp.where(lane == 0, 0.0, pltpu.roll(q, 1, 1))
                qn = jnp.where(lane == lats - 1, 0.0, pltpu.roll(q, lats - 1, 1))
                r = q - flows[0] * (q - qw)
                r = r - flows[1] * (qe - q)
                r = r - flows[2] * (q - qs)
                q = r - flows[3] * (qn - q)
            inner = q[4 : 4 + width, :]
            prior[m * layers + l] = inner
            for h in range(halves):
                cols[h, pl.ds(l * mem_dev + m, width, stride=rows), :] = inner[
                    :, h * 128 : (h + 1) * 128
                ]
            return total + inner

        total = lax.fori_loop(
            0, mem_dev, step, jnp.zeros((width, lats), jnp.float32), unroll=2
        )
        partial[me_mem, l] = total

    mean_copies = [
        send(partial.at[me_mem], partial.at[me_mem], mean_send.at[d], mean_recv.at[d], peer)
        for d, peer in enumerate(others)
    ]

    def turn(g, carry):
        for u in range(4):
            i = g * 4 + u
            blocks = [cols[h, pl.ds(pl.multiple_of(i * rows, 8), rows), :].T for h in range(halves)]
            for h in range(halves):
                table[pl.ds(pl.multiple_of(i * lats + h * 128, 128), 128), 0:rows] = blocks[h]
        return carry

    lax.fori_loop(0, width // 4, turn, 0)

    slots = within.shape[0]
    unroll = 32
    chunks = obs_send.shape[0]
    chunk = slots // chunks

    def fetch(g, carry):
        found = [table[pl.ds(within[g * unroll + u], 1), :] for u in range(unroll)]
        for u in range(unroll):
            picked[pl.ds(g * unroll + u, 1), :] = found[u]
        return carry

    def sort_out(c, carry):
        start = pl.multiple_of(c * 128, 128)
        block = picked[pl.ds(start, 128), :].T
        lev = level[:, pl.ds(start, 128)]
        value = block[0:mem_dev]
        for l in range(1, layers):
            value = jnp.where(lev == l, block[l * mem_dev : (l + 1) * mem_dev], value)
        gathered[me_mem, :, pl.ds(start, 128)] = value
        obs_horiz[:, pl.ds(start, 128)] = block[stack : stack + 8]
        return carry

    obs_copies = []
    for c in range(chunks):
        lax.fori_loop(c * chunk // unroll, (c + 1) * chunk // unroll, fetch, 0)
        lax.fori_loop(c * chunk // 128, (c + 1) * chunk // 128, sort_out, 0, unroll=True)
        piece = gathered.at[me_mem, :, pl.ds(c * chunk, chunk)]
        for d, peer in enumerate(others):
            obs_copies.append(send(piece, piece, obs_send.at[c, d], obs_recv.at[c, d], peer))
    for copy in mean_copies:
        copy.wait_recv()
    field = partial[0]
    for g in range(1, n_mem):
        field = field + partial[g]
    mean[...] = field / (n_mem * mem_dev)
    for copy in obs_copies:
        copy.wait_recv()
    obs_prior[...] = gathered[...]
    to_left.wait_send()
    to_right.wait_send()
    for copy in mean_copies + obs_copies:
        copy.wait_send()


def gram_kernel(
    n_lon, n_mem, mem_dev, norm,
    obs_prior, obs_horiz, level, vert, count, value, var,
    system,
    perts, weighted, staged, heard, whole,
    part_send, part_recv, lon_send, lon_recv, mem_send, mem_recv,
):
    slots = level.shape[1]
    layers = vert.shape[1]
    total = n_mem * mem_dev
    local = mem_dev * MODES
    size = total * MODES
    me = lax.axis_index("lon")
    me_mem = lax.axis_index("mem")
    lon_peers = axis_peers("lon", n_lon)
    mem_peers = axis_peers("mem", n_mem)

    barrier = greet(lon_peers + mem_peers)
    lev = level[...]
    states = obs_prior[...].reshape(total, slots)
    centre = jnp.sum(states, axis=0, keepdims=True) / total
    slot = lax.broadcasted_iota(jnp.int32, (1, slots), 1)
    live = jnp.where(slot < count[0], 1.0, 0.0)
    inv_var = live / var[...]
    drive = inv_var * (value[...] - centre)
    scale = live * norm
    vert_obs = []
    for a in range(KV):
        v = jnp.full((1, slots), vert[a, 0])
        for l in range(1, layers):
            v = jnp.where(lev == l, vert[a, l], v)
        vert_obs.append(jnp.broadcast_to(v, (KH, slots)))
    modes = jnp.concatenate(vert_obs, axis=0) * obs_horiz[...]
    for g in range(n_mem):
        for m in range(mem_dev):
            row = (g * mem_dev + m) * MODES
            anomaly = obs_prior[g, m : m + 1, :] - centre
            perts[row : row + MODES, :] = anomaly * modes * scale
    start = pl.multiple_of(me_mem * local, local)
    mine = perts[pl.ds(start, local), :]
    weighted[...] = mine * inv_var
    gram = lax.dot_general(
        weighted[...], perts[...], (((1,), (1,)), ((), ())),
        precision=HIGHEST, preferred_element_type=jnp.float32,
    )
    side = jnp.sum(mine * drive, axis=1, keepdims=True)
    for d in range(n_lon):
        staged[d, :, 0:size] = gram[d * 8 : (d + 1) * 8]
        staged[d, :, size : size + 128] = jnp.broadcast_to(side[d * 8 : (d + 1) * 8], (8, 128))

    pl.semaphore_wait(barrier, len(lon_peers) + len(mem_peers))
    parts = []
    for d, peer in enumerate(lon_peers):
        parts.append(
            send(staged.at[peer["lon"]], heard.at[me], part_send.at[d], part_recv.at[d], peer)
        )
    heard[me] = staged[me]
    for copy in parts:
        copy.wait_recv()
    block = heard[0]
    for d in range(1, n_lon):
        block = block + heard[d]
    whole[me_mem, me] = block
    spread = [
        send(whole.at[me_mem, me], whole.at[me_mem, me], lon_send.at[d], lon_recv.at[d], peer)
        for d, peer in enumerate(lon_peers)
    ]
    for copy in spread:
        copy.wait_recv()
    across = [
        send(whole.at[me_mem], whole.at[me_mem], mem_send.at[d], mem_recv.at[d], peer)
        for d, peer in enumerate(mem_peers)
    ]
    for copy in across:
        copy.wait_recv()
    system[...] = whole[...].reshape(size, size + 128)
    for copy in parts + spread + across:
        copy.wait_send()


def solve_kernel(system, prior, weights, prior_out, work, copy_sem):
    size, columns = system.shape
    keep = pltpu.make_async_copy(prior, prior_out, copy_sem)
    keep.start()
    row = lax.broadcasted_iota(jnp.int32, (size, columns), 0)
    col = lax.broadcasted_iota(jnp.int32, (size, columns), 1)
    work[...] = system[...] + jnp.where(row == col, 1.0, 0.0)
    depth = 64
    tile = (8, 128)
    sub = lax.broadcasted_iota(jnp.int32, tile, 0)
    outer = lax.broadcasted_iota(jnp.int32, (size, depth), 0)
    for top in range(0, size, depth):
        low = top // 128 * 128
        pieces = (columns - low) // 128
        panel = [
            [work[top + i * 8 : top + i * 8 + 8, low + k * 128 : low + (k + 1) * 128] for k in range(pieces)]
            for i in range(depth // 8)
        ]
        for s in range(depth // 8):
            lane = top - low + s * 8
            a = [jnp.broadcast_to(panel[s][0][:, lane + c : lane + c + 1], tile) for c in range(8)]
            rows = panel[s]
            for j in range(8):
                inv = 1.0 / jnp.broadcast_to(a[j][j : j + 1], tile)
                f = a[j]

                def reduce(x, j=j, inv=inv, f=f):
                    n = jnp.broadcast_to(x[j : j + 1], tile) * inv
                    return jnp.where(sub == j, n, x - f * n)

                for c in range(j + 1, 8):
                    a[c] = reduce(a[c])
                rows = [reduce(x) for x in rows]
            panel[s] = rows
            spread = [[jnp.broadcast_to(x[j : j + 1], tile) for x in rows] for j in range(8)]
            for d in range(1, depth // 8):
                i = (s + d) % (depth // 8)
                lead = panel[i][0]
                block = panel[i]
                for j in range(8):
                    f = jnp.broadcast_to(lead[:, lane + j : lane + j + 1], tile)
                    block = [x - f * y for x, y in zip(block, spread[j])]
                panel[i] = block
        for i in range(depth // 8):
            for k in range(pieces):
                work[top + i * 8 : top + i * 8 + 8, low + k * 128 : low + (k + 1) * 128] = panel[i][k]
        inside = (outer >= top) & (outer < top + depth)
        factor = jnp.where(inside, 0.0, work[:, top : top + depth])
        first = (top + depth) // 128 * 128
        work[:, first:columns] -= jnp.dot(
            factor, work[top : top + depth, first:columns],
            precision=HIGHEST, preferred_element_type=jnp.float32,
        )
    weights[...] = work[:, size : size + 128]
    keep.wait()


def analysis_kernel(
    n_mem, mem_dev, norm,
    weights, prior, mean, horiz, vert,
    analysis,
    partial, part_send, part_recv,
):
    layers = vert.shape[1]
    lats = mean.shape[2]
    me_mem = lax.axis_index("mem")
    peers = axis_peers("mem", n_mem)
    barrier = greet(peers)
    copies = []
    for l in range(layers):
        centre = mean[l]
        total = jnp.zeros_like(centre)
        for m in range(mem_dev):
            start = pl.multiple_of((me_mem * mem_dev + m) * MODES, 8)
            w = weights[pl.ds(start, MODES), :]
            mixed = vert[0, l] * w[0:KH] + vert[1, l] * w[KH : 2 * KH]
            mixed = jnp.concatenate([mixed] * (lats // 128), axis=1)
            coef = mixed[0:1] * horiz[0]
            for b in range(1, KH):
                coef = coef + mixed[b : b + 1] * horiz[b]
            total = total + coef * (prior[m * layers + l] - centre)
        partial[me_mem, l] = total
        if l == 0:
            pl.semaphore_wait(barrier, len(peers))
        piece = partial.at[me_mem, l]
        for d, peer in enumerate(peers):
            copies.append(send(piece, piece, part_send.at[l, d], part_recv.at[l, d], peer))
    for l in range(layers):
        for copy in copies[l * len(peers) : (l + 1) * len(peers)]:
            copy.wait_recv()
        field = partial[0, l]
        for g in range(1, n_mem):
            field = field + partial[g, l]
        analysis[l] = mean[l] + field * norm
    for copy in copies:
        copy.wait_send()


def params(collective=None):
    if collective is None:
        return pltpu.CompilerParams(vmem_limit_bytes=VMEM_LIMIT)
    return pltpu.CompilerParams(
        vmem_limit_bytes=VMEM_LIMIT, collective_id=collective, has_side_effects=True
    )


def fast_device(
    members, courant_lon, courant_lat, vert_modes, horiz_modes,
    obs_index, obs_count, obs_value, obs_var,
):
    f32 = jnp.float32
    mem_dev, layers, width, lats = members.shape
    n_lon = lax.axis_size("lon")
    n_mem = lax.axis_size("mem")
    total = mem_dev * n_mem
    size = total * MODES
    norm = (total - 1) ** (-0.5)
    slots = obs_index.shape[0]
    stack = mem_dev * layers
    cells = width * lats
    level = sum((obs_index >= l * cells).astype(jnp.int32) for l in range(1, layers))
    within = obs_index - cells * level
    level = level.reshape(1, slots)
    dma = pltpu.SemaphoreType.DMA
    halves = lats // 128
    edge_rows = 2 * stack + 2 * layers
    prior, mean, obs_prior, obs_horiz = pl.pallas_call(
        functools.partial(advect_kernel, n_lon, n_mem, mem_dev),
        out_shape=(
            jax.ShapeDtypeStruct((stack, width, lats), f32),
            jax.ShapeDtypeStruct((layers, width, lats), f32),
            jax.ShapeDtypeStruct((n_mem, mem_dev, slots), f32),
            jax.ShapeDtypeStruct((8, slots), f32),
        ),
        in_specs=[vmem()] * 5 + [smem()],
        out_specs=(vmem(),) * 4,
        scratch_shapes=[
            pltpu.VMEM((2, edge_rows, lats), f32),
            pltpu.VMEM((2, edge_rows, lats), f32),
            pltpu.VMEM((stack, width + 8, lats), f32),
            pltpu.VMEM((layers, width + 8, lats), f32),
            pltpu.VMEM((layers, width + 8, lats), f32),
            pltpu.VMEM((n_mem, layers, width, lats), f32),
            pltpu.VMEM((halves, width * 40, 128), f32),
            pltpu.VMEM((cells, 128), f32),
            pltpu.VMEM((slots, 128), f32),
            pltpu.VMEM((n_mem, mem_dev, slots), f32),
            dma((2,)), dma((2,)),
            dma((n_mem - 1,)), dma((n_mem - 1,)),
            dma((4, n_mem - 1)), dma((4, n_mem - 1)),
        ],
        compiler_params=params(1),
        name="advect",
    )(members.reshape(stack, width, lats), courant_lon, courant_lat, horiz_modes, level, within)
    system = pl.pallas_call(
        functools.partial(gram_kernel, n_lon, n_mem, mem_dev, norm),
        out_shape=jax.ShapeDtypeStruct((size, size + 128), f32),
        in_specs=[vmem()] * 3 + [smem()] * 2 + [vmem()] * 2,
        out_specs=vmem(),
        scratch_shapes=[
            pltpu.VMEM((size, slots), f32),
            pltpu.VMEM((mem_dev * MODES, slots), f32),
            pltpu.VMEM((n_lon, 8, size + 128), f32),
            pltpu.VMEM((n_lon, 8, size + 128), f32),
            pltpu.VMEM((n_mem, n_lon, 8, size + 128), f32),
            dma((n_lon - 1,)), dma((n_lon - 1,)),
            dma((n_lon - 1,)), dma((n_lon - 1,)),
            dma((n_mem - 1,)), dma((n_mem - 1,)),
        ],
        compiler_params=params(2),
        name="gram",
    )(
        obs_prior, obs_horiz, level, vert_modes, obs_count,
        obs_value.reshape(1, slots), obs_var.reshape(1, slots),
    )
    anywhere = pl.BlockSpec(memory_space=pl.ANY)
    weights, prior_out = pl.pallas_call(
        solve_kernel,
        out_shape=(
            jax.ShapeDtypeStruct((size, 128), f32),
            jax.ShapeDtypeStruct(prior.shape, f32),
        ),
        in_specs=[vmem(), vmem()],
        out_specs=(vmem(), anywhere),
        scratch_shapes=[pltpu.VMEM((size, size + 128), f32), dma],
        compiler_params=params(),
        name="solve",
    )(system, prior)
    analysis = pl.pallas_call(
        functools.partial(analysis_kernel, n_mem, mem_dev, norm),
        out_shape=jax.ShapeDtypeStruct((layers, width, lats), f32),
        in_specs=[vmem()] * 4 + [smem()],
        out_specs=vmem(),
        scratch_shapes=[
            pltpu.VMEM((n_mem, layers, width, lats), f32),
            dma((layers, n_mem - 1)), dma((layers, n_mem - 1)),
        ],
        compiler_params=params(3),
        name="analysis",
    )(weights, prior, mean, horiz_modes, vert_modes)
    return prior_out.reshape(members.shape), analysis


def padded(block, sides, width):
    for axis, dim in sides:
        count = lax.axis_size(axis)
        forward = [(i, i + 1) for i in range(count - 1)]
        forward.append((count - 1, 0))
        backward = [(target, source) for source, target in forward]
        low = lax.ppermute(
            lax.slice_in_dim(block, block.shape[dim] - width, None, axis=dim), axis, forward
        )
        high = lax.ppermute(lax.slice_in_dim(block, 0, width, axis=dim), axis, backward)
        block = jnp.concatenate([low, block, high], axis=dim)
    return block


def update(centre, western, eastern, flow_lon, flow_lat):
    zero_col = jnp.zeros_like(centre[..., :1])
    south_boundary = jnp.concatenate([zero_col, centre[..., :-1]], axis=-1)
    northern = jnp.concatenate([centre[..., 1:], zero_col], axis=-1)
    result = centre - jnp.maximum(flow_lon, 0.0) * (centre - western)
    result = result - jnp.minimum(flow_lon, 0.0) * (eastern - centre)
    result = result - jnp.maximum(flow_lat, 0.0) * (centre - south_boundary)
    result = result - jnp.minimum(flow_lat, 0.0) * (northern - centre)
    return result


def per_device(
    members,
    courant_lon,
    courant_lat,
    vert_modes,
    horiz_modes,
    obs_index,
    obs_count,
    obs_value,
    obs_var,
):
    mem_dev, layer_tally, band_width, lat_rows = members.shape
    sample_tally_overall = mem_dev * lax.axis_size("mem")
    rim_depth = ADV_STEPS
    stacked = jnp.concatenate(
        [members.reshape(mem_dev * layer_tally, band_width, lat_rows), courant_lon, courant_lat],
        axis=0,
    )
    extended = padded(stacked, (("lon", 1),), rim_depth)
    split_at = mem_dev * layer_tally
    prognostic_vector = extended[:split_at].reshape(
        mem_dev, layer_tally, band_width + 2 * rim_depth, lat_rows
    )
    flow_lon_ext = extended[split_at : split_at + layer_tally]
    meridional_wind_padded = extended[split_at + layer_tally :]
    for section in range(rim_depth):
        out_cols = band_width + 2 * (rim_depth - 1 - section)
        first_col = section + 1
        prognostic_vector = update(
            prognostic_vector[:, :, 1 : out_cols + 1],
            prognostic_vector[:, :, 0:out_cols],
            prognostic_vector[:, :, 2 : out_cols + 2],
            flow_lon_ext[:, first_col : first_col + out_cols],
            meridional_wind_padded[:, first_col : first_col + out_cols],
        )
    sample_centroid = lax.psum(jnp.sum(prognostic_vector, axis=0), "mem") / sample_tally_overall
    sample_departure = prognostic_vector - sample_centroid[None]
    norm_scale = (sample_tally_overall - 1) ** (-0.5)
    obs_slots = obs_index.shape[0]
    band_cells = band_width * lat_rows
    level_idx = obs_index // band_cells
    within = obs_index % band_cells
    anomaly_obs = jnp.take(sample_departure.reshape(mem_dev, -1), obs_index, axis=1)
    mean_obs = jnp.take(sample_centroid.reshape(-1), obs_index)
    vert_obs = jnp.take(vert_modes, level_idx, axis=1)
    horiz_obs = jnp.take(horiz_modes.reshape(KH, -1), within, axis=1)
    modes_obs = (vert_obs[:, None, :] * horiz_obs[None, :, :]).reshape(KV * KH, obs_slots)
    live_mask = (jnp.arange(obs_slots, dtype=jnp.int32) < obs_count[0]).astype(jnp.float32)
    obs_perts = (
        anomaly_obs[:, None, :] * modes_obs[None, :, :] * (live_mask * norm_scale)[None, None, :]
    )
    obs_perts = obs_perts.reshape(mem_dev * KV * KH, obs_slots)
    inv_var = live_mask / obs_var
    innovation = obs_value - mean_obs
    all_perts = lax.all_gather(obs_perts, "mem", axis=0, tiled=True)
    gram_part = jnp.dot(all_perts * inv_var[None, :], all_perts.T, precision=lax.Precision.HIGHEST)
    side_part = jnp.dot(all_perts, inv_var * innovation, precision=lax.Precision.HIGHEST)
    gram_matrix, right_side = lax.psum((gram_part, side_part), "lon")
    system = jnp.eye(gram_matrix.shape[0], dtype=jnp.float32) + gram_matrix
    factor = jnp.linalg.cholesky(system)
    weights = jax.scipy.linalg.cho_solve((factor, True), right_side)
    w_mat = weights.reshape(sample_tally_overall, KV * KH)
    w_local = lax.dynamic_slice_in_dim(w_mat, lax.axis_index("mem") * mem_dev, mem_dev, 0)
    mode_coef = jnp.einsum(
        "mk,mlij->klij", w_local, sample_departure, precision=lax.Precision.HIGHEST
    )
    mode_coef = mode_coef.reshape(KV, KH, layer_tally, band_width, lat_rows)
    inc_part = (
        jnp.einsum(
            "al,bij,ablij->lij", vert_modes, horiz_modes, mode_coef, precision=lax.Precision.HIGHEST
        )
        * norm_scale
    )
    posterior_adjustment = lax.psum(inc_part, "mem")
    return (prognostic_vector, sample_centroid + posterior_adjustment)


def choose(*args):
    mem_dev, layers, width, lats = args[0].shape
    n_lon = lax.axis_size("lon")
    fits = (
        mem_dev == 8
        and layers == 4
        and width % 8 == 0
        and lats % 128 == 0
        and args[5].shape[0] % 512 == 0
        and n_lon > 2
        and mem_dev * MODES == 8 * n_lon
        and (mem_dev * lax.axis_size("mem") * MODES) % 128 == 0
    )
    return fast_device(*args) if fits else per_device(*args)


def solution(mesh):
    placed = (
        P("mem", None, "lon", None),
        P(None, "lon", None),
        P(None, "lon", None),
        P(),
        P(None, "lon", None),
        P("lon"),
        P("lon"),
        P("lon"),
        P("lon"),
    )
    return jax.shard_map(
        choose,
        mesh=mesh,
        in_specs=placed,
        out_specs=(P("mem", None, "lon", None), P(None, "lon", None)),
        check_vma=False,
    )
```

```python
import functools

import jax
import jax.numpy as jnp
from jax import lax
from jax.experimental import pallas as pl
from jax.experimental.pallas import tpu as pltpu
from jax.sharding import PartitionSpec as P

KV = 2
KH = 4
ADV_STEPS = 2
MODES = KV * KH
MESH = pl.DeviceIdType.MESH
VMEM_LIMIT = 20 * 1024 * 1024
HIGHEST = lax.Precision.HIGHEST


def vmem():
    return pl.BlockSpec(memory_space=pltpu.VMEM)


def smem():
    return pl.BlockSpec(memory_space=pltpu.SMEM)


def greet(peers):
    barrier = pltpu.get_barrier_semaphore()
    for peer in peers:
        pl.semaphore_signal(barrier, inc=1, device_id=peer, device_id_type=MESH)
    return barrier


def axis_peers(axis, count):
    me = lax.axis_index(axis)
    return [{axis: lax.rem(me + d, count)} for d in range(1, count)]


def send(src, dst, send_sem, recv_sem, peer):
    copy = pltpu.make_async_remote_copy(
        src_ref=src, dst_ref=dst, send_sem=send_sem, recv_sem=recv_sem,
        device_id=peer, device_id_type=MESH,
    )
    copy.start()
    return copy


def advect_kernel(
    n_lon, n_mem, mem_dev,
    members, cx, cy, horiz, level, within,
    prior, mean, obs_prior, obs_horiz,
    edge_out, edge_in, ext, cx_ext, cy_ext, partial, cols, table, picked, gathered,
    edge_send, edge_recv, mean_send, mean_recv, obs_send, obs_recv,
):
    layers = cx.shape[0]
    stack, width, lats = members.shape
    rows = 40
    halves = lats // 128
    me = lax.axis_index("lon")
    me_mem = lax.axis_index("mem")
    left = {"lon": lax.rem(me + n_lon - 1, n_lon)}
    right = {"lon": lax.rem(me + 1, n_lon)}
    others = axis_peers("mem", n_mem)

    barrier = greet([left, right] + others)
    for side, (first, second, rim) in enumerate(((0, 1, 0), (width - 2, width - 1, width - 1))):
        edge_out[side, 0:stack, :] = members[:, first, :]
        edge_out[side, stack : 2 * stack, :] = members[:, second, :]
        edge_out[side, 2 * stack : 2 * stack + layers, :] = cx[:, rim, :]
        edge_out[side, 2 * stack + layers : 2 * stack + 2 * layers, :] = cy[:, rim, :]
    pl.semaphore_wait(barrier, 2 + len(others))
    to_left = send(edge_out.at[0], edge_in.at[1], edge_send.at[0], edge_recv.at[1], left)
    to_right = send(edge_out.at[1], edge_in.at[0], edge_send.at[1], edge_recv.at[0], right)

    ext[:, 4 : 4 + width, :] = members[...]
    cx_ext[:, 4 : 4 + width, :] = cx[...]
    cy_ext[:, 4 : 4 + width, :] = cy[...]
    for b in range(2 * KH):
        for h in range(halves):
            cols[h, pl.ds(stack + b, width, stride=rows), :] = horiz[
                b % KH, :, h * 128 : (h + 1) * 128
            ]
    to_left.wait_recv()
    to_right.wait_recv()
    high = 4 + width
    ext[:, 2, :] = edge_in[0, 0:stack, :]
    ext[:, 3, :] = edge_in[0, stack : 2 * stack, :]
    ext[:, high, :] = edge_in[1, 0:stack, :]
    ext[:, high + 1, :] = edge_in[1, stack : 2 * stack, :]
    for side, row in ((0, 3), (1, high)):
        cx_ext[:, row, :] = edge_in[side, 2 * stack : 2 * stack + layers, :]
        cy_ext[:, row, :] = edge_in[side, 2 * stack + layers : 2 * stack + 2 * layers, :]

    ext_rows = width + 8
    lane = lax.broadcasted_iota(jnp.int32, (ext_rows, lats), 1)
    for l in range(layers):
        cx_l = cx_ext[l]
        cy_l = cy_ext[l]
        east_flow = jnp.maximum(cx_l, 0.0)
        west_flow = jnp.minimum(cx_l, 0.0)
        north_flow = jnp.maximum(cy_l, 0.0)
        south_flow = jnp.minimum(cy_l, 0.0)

        def step(m, total, l=l, flows=(east_flow, west_flow, north_flow, south_flow)):
            q = ext[m * layers + l]
            for _ in range(ADV_STEPS):
                qw = pltpu.roll(q, 1, 0)
                qe = pltpu.roll(q, ext_rows - 1, 0)
                qs = jnp.where(lane == 0, 0.0, pltpu.roll(q, 1, 1))
                qn = jnp.where(lane == lats - 1, 0.0, pltpu.roll(q, lats - 1, 1))
                r = q - flows[0] * (q - qw)
                r = r - flows[1] * (qe - q)
                r = r - flows[2] * (q - qs)
                q = r - flows[3] * (qn - q)
            inner = q[4 : 4 + width, :]
            prior[m * layers + l] = inner
            for h in range(halves):
                cols[h, pl.ds(l * mem_dev + m, width, stride=rows), :] = inner[
                    :, h * 128 : (h + 1) * 128
                ]
            return total + inner

        total = lax.fori_loop(
            0, mem_dev, step, jnp.zeros((width, lats), jnp.float32), unroll=4
        )
        partial[me_mem, l] = total

    mean_copies = [
        send(partial.at[me_mem], partial.at[me_mem], mean_send.at[d], mean_recv.at[d], peer)
        for d, peer in enumerate(others)
    ]

    def turn(g, carry):
        for u in range(8):
            i = g * 8 + u
            blocks = [cols[h, pl.ds(pl.multiple_of(i * rows, 8), rows), :].T for h in range(halves)]
            for h in range(halves):
                table[pl.ds(pl.multiple_of(i * lats + h * 128, 128), 128), 0:rows] = blocks[h]
        return carry

    lax.fori_loop(0, width // 8, turn, 0)

    slots = within.shape[0]
    unroll = 32
    chunks = obs_send.shape[0]
    chunk = slots // chunks

    def fetch(g, carry):
        found = [table[pl.ds(within[g * unroll + u], 1), :] for u in range(unroll)]
        for u in range(unroll):
            picked[pl.ds(g * unroll + u, 1), :] = found[u]
        return carry

    def sort_out(c, carry):
        start = pl.multiple_of(c * 128, 128)
        block = picked[pl.ds(start, 128), :].T
        lev = level[:, pl.ds(start, 128)]
        value = block[0:mem_dev]
        for l in range(1, layers):
            value = jnp.where(lev == l, block[l * mem_dev : (l + 1) * mem_dev], value)
        gathered[me_mem, :, pl.ds(start, 128)] = value
        obs_horiz[:, pl.ds(start, 128)] = block[stack : stack + 8]
        return carry

    obs_copies = []
    for c in range(chunks):
        lax.fori_loop(c * chunk // unroll, (c + 1) * chunk // unroll, fetch, 0)
        lax.fori_loop(c * chunk // 128, (c + 1) * chunk // 128, sort_out, 0, unroll=True)
        piece = gathered.at[me_mem, :, pl.ds(c * chunk, chunk)]
        for d, peer in enumerate(others):
            obs_copies.append(send(piece, piece, obs_send.at[c, d], obs_recv.at[c, d], peer))
    for copy in mean_copies:
        copy.wait_recv()
    field = partial[0]
    for g in range(1, n_mem):
        field = field + partial[g]
    mean[...] = field / (n_mem * mem_dev)
    for copy in obs_copies:
        copy.wait_recv()
    obs_prior[...] = gathered[...]
    to_left.wait_send()
    to_right.wait_send()
    for copy in mean_copies + obs_copies:
        copy.wait_send()


def gram_kernel(
    n_lon, n_mem, mem_dev, norm,
    obs_prior, obs_horiz, level, vert, count, value, var,
    system,
    perts, weighted, staged, heard, whole,
    part_send, part_recv, lon_send, lon_recv, mem_send, mem_recv,
):
    slots = level.shape[1]
    layers = vert.shape[1]
    total = n_mem * mem_dev
    local = mem_dev * MODES
    size = total * MODES
    me = lax.axis_index("lon")
    me_mem = lax.axis_index("mem")
    lon_peers = axis_peers("lon", n_lon)
    mem_peers = axis_peers("mem", n_mem)

    barrier = greet(lon_peers + mem_peers)
    lev = level[...]
    states = obs_prior[...].reshape(total, slots)
    centre = jnp.sum(states, axis=0, keepdims=True) / total
    slot = lax.broadcasted_iota(jnp.int32, (1, slots), 1)
    live = jnp.where(slot < count[0], 1.0, 0.0)
    inv_var = live / var[...]
    drive = inv_var * (value[...] - centre)
    scale = live * norm
    vert_obs = []
    for a in range(KV):
        v = jnp.full((1, slots), vert[a, 0])
        for l in range(1, layers):
            v = jnp.where(lev == l, vert[a, l], v)
        vert_obs.append(jnp.broadcast_to(v, (KH, slots)))
    modes = jnp.concatenate(vert_obs, axis=0) * obs_horiz[...]
    for g in range(n_mem):
        for m in range(mem_dev):
            row = (g * mem_dev + m) * MODES
            anomaly = obs_prior[g, m : m + 1, :] - centre
            perts[row : row + MODES, :] = anomaly * modes * scale
    start = pl.multiple_of(me_mem * local, local)
    mine = perts[pl.ds(start, local), :]
    weighted[...] = mine * inv_var
    gram = lax.dot_general(
        weighted[...], perts[...], (((1,), (1,)), ((), ())),
        precision=HIGHEST, preferred_element_type=jnp.float32,
    )
    side = jnp.sum(mine * drive, axis=1, keepdims=True)
    for d in range(n_lon):
        staged[d, :, 0:size] = gram[d * 8 : (d + 1) * 8]
        staged[d, :, size : size + 128] = jnp.broadcast_to(side[d * 8 : (d + 1) * 8], (8, 128))

    pl.semaphore_wait(barrier, len(lon_peers) + len(mem_peers))
    parts = []
    for d, peer in enumerate(lon_peers):
        parts.append(
            send(staged.at[peer["lon"]], heard.at[me], part_send.at[d], part_recv.at[d], peer)
        )
    heard[me] = staged[me]
    for copy in parts:
        copy.wait_recv()
    block = heard[0]
    for d in range(1, n_lon):
        block = block + heard[d]
    whole[me_mem, me] = block
    spread = [
        send(whole.at[me_mem, me], whole.at[me_mem, me], lon_send.at[d], lon_recv.at[d], peer)
        for d, peer in enumerate(lon_peers)
    ]
    for copy in spread:
        copy.wait_recv()
    across = [
        send(whole.at[me_mem], whole.at[me_mem], mem_send.at[d], mem_recv.at[d], peer)
        for d, peer in enumerate(mem_peers)
    ]
    for copy in across:
        copy.wait_recv()
    system[...] = whole[...].reshape(size, size + 128)
    for copy in parts + spread + across:
        copy.wait_send()


def solve_kernel(system, prior, weights, prior_out, work, copy_sem):
    size, columns = system.shape
    keep = pltpu.make_async_copy(prior, prior_out, copy_sem)
    keep.start()
    row = lax.broadcasted_iota(jnp.int32, (size, columns), 0)
    col = lax.broadcasted_iota(jnp.int32, (size, columns), 1)
    work[...] = system[...] + jnp.where(row == col, 1.0, 0.0)
    depth = 64
    tile = (8, 128)
    sub = lax.broadcasted_iota(jnp.int32, tile, 0)
    outer = lax.broadcasted_iota(jnp.int32, (size, depth), 0)
    for top in range(0, size, depth):
        low = top // 128 * 128
        pieces = (columns - low) // 128
        panel = [
            [work[top + i * 8 : top + i * 8 + 8, low + k * 128 : low + (k + 1) * 128] for k in range(pieces)]
            for i in range(depth // 8)
        ]
        for s in range(depth // 8):
            lane = top - low + s * 8
            a = [jnp.broadcast_to(panel[s][0][:, lane + c : lane + c + 1], tile) for c in range(8)]
            rows = panel[s]
            for j in range(8):
                inv = 1.0 / jnp.broadcast_to(a[j][j : j + 1], tile)
                f = a[j]

                def reduce(x, j=j, inv=inv, f=f):
                    n = jnp.broadcast_to(x[j : j + 1], tile) * inv
                    return jnp.where(sub == j, n, x - f * n)

                for c in range(j + 1, 8):
                    a[c] = reduce(a[c])
                rows = [reduce(x) for x in rows]
            panel[s] = rows
            spread = [[jnp.broadcast_to(x[j : j + 1], tile) for x in rows] for j in range(8)]
            for d in range(1, depth // 8):
                i = (s + d) % (depth // 8)
                lead = panel[i][0]
                block = panel[i]
                for j in range(8):
                    f = jnp.broadcast_to(lead[:, lane + j : lane + j + 1], tile)
                    block = [x - f * y for x, y in zip(block, spread[j])]
                panel[i] = block
        for i in range(depth // 8):
            for k in range(pieces):
                work[top + i * 8 : top + i * 8 + 8, low + k * 128 : low + (k + 1) * 128] = panel[i][k]
        inside = (outer >= top) & (outer < top + depth)
        factor = jnp.where(inside, 0.0, work[:, top : top + depth])
        first = (top + depth) // 128 * 128
        work[:, first:columns] -= jnp.dot(
            factor, work[top : top + depth, first:columns],
            precision=HIGHEST, preferred_element_type=jnp.float32,
        )
    weights[...] = work[:, size : size + 128]
    keep.wait()


def analysis_kernel(
    n_mem, mem_dev, norm,
    weights, prior, mean, horiz, vert,
    analysis,
    partial, part_send, part_recv,
):
    layers = vert.shape[1]
    lats = mean.shape[2]
    me_mem = lax.axis_index("mem")
    peers = axis_peers("mem", n_mem)
    barrier = greet(peers)
    copies = []
    for l in range(layers):
        centre = mean[l]
        total = jnp.zeros_like(centre)
        for m in range(mem_dev):
            start = pl.multiple_of((me_mem * mem_dev + m) * MODES, 8)
            w = weights[pl.ds(start, MODES), :]
            mixed = vert[0, l] * w[0:KH] + vert[1, l] * w[KH : 2 * KH]
            mixed = jnp.concatenate([mixed] * (lats // 128), axis=1)
            coef = mixed[0:1] * horiz[0]
            for b in range(1, KH):
                coef = coef + mixed[b : b + 1] * horiz[b]
            total = total + coef * (prior[m * layers + l] - centre)
        partial[me_mem, l] = total
        if l == 0:
            pl.semaphore_wait(barrier, len(peers))
        piece = partial.at[me_mem, l]
        for d, peer in enumerate(peers):
            copies.append(send(piece, piece, part_send.at[l, d], part_recv.at[l, d], peer))
    for l in range(layers):
        for copy in copies[l * len(peers) : (l + 1) * len(peers)]:
            copy.wait_recv()
        field = partial[0, l]
        for g in range(1, n_mem):
            field = field + partial[g, l]
        analysis[l] = mean[l] + field * norm
    for copy in copies:
        copy.wait_send()


def params(collective=None):
    if collective is None:
        return pltpu.CompilerParams(vmem_limit_bytes=VMEM_LIMIT)
    return pltpu.CompilerParams(
        vmem_limit_bytes=VMEM_LIMIT, collective_id=collective, has_side_effects=True
    )


def fast_device(
    members, courant_lon, courant_lat, vert_modes, horiz_modes,
    obs_index, obs_count, obs_value, obs_var,
):
    f32 = jnp.float32
    mem_dev, layers, width, lats = members.shape
    n_lon = lax.axis_size("lon")
    n_mem = lax.axis_size("mem")
    total = mem_dev * n_mem
    size = total * MODES
    norm = (total - 1) ** (-0.5)
    slots = obs_index.shape[0]
    stack = mem_dev * layers
    cells = width * lats
    level = sum((obs_index >= l * cells).astype(jnp.int32) for l in range(1, layers))
    within = obs_index - cells * level
    level = level.reshape(1, slots)
    dma = pltpu.SemaphoreType.DMA
    halves = lats // 128
    edge_rows = 2 * stack + 2 * layers
    prior, mean, obs_prior, obs_horiz = pl.pallas_call(
        functools.partial(advect_kernel, n_lon, n_mem, mem_dev),
        out_shape=(
            jax.ShapeDtypeStruct((stack, width, lats), f32),
            jax.ShapeDtypeStruct((layers, width, lats), f32),
            jax.ShapeDtypeStruct((n_mem, mem_dev, slots), f32),
            jax.ShapeDtypeStruct((8, slots), f32),
        ),
        in_specs=[vmem()] * 5 + [smem()],
        out_specs=(vmem(),) * 4,
        scratch_shapes=[
            pltpu.VMEM((2, edge_rows, lats), f32),
            pltpu.VMEM((2, edge_rows, lats), f32),
            pltpu.VMEM((stack, width + 8, lats), f32),
            pltpu.VMEM((layers, width + 8, lats), f32),
            pltpu.VMEM((layers, width + 8, lats), f32),
            pltpu.VMEM((n_mem, layers, width, lats), f32),
            pltpu.VMEM((halves, width * 40, 128), f32),
            pltpu.VMEM((cells, 128), f32),
            pltpu.VMEM((slots, 128), f32),
            pltpu.VMEM((n_mem, mem_dev, slots), f32),
            dma((2,)), dma((2,)),
            dma((n_mem - 1,)), dma((n_mem - 1,)),
            dma((4, n_mem - 1)), dma((4, n_mem - 1)),
        ],
        compiler_params=params(1),
        name="advect",
    )(members.reshape(stack, width, lats), courant_lon, courant_lat, horiz_modes, level, within)
    system = pl.pallas_call(
        functools.partial(gram_kernel, n_lon, n_mem, mem_dev, norm),
        out_shape=jax.ShapeDtypeStruct((size, size + 128), f32),
        in_specs=[vmem()] * 3 + [smem()] * 2 + [vmem()] * 2,
        out_specs=vmem(),
        scratch_shapes=[
            pltpu.VMEM((size, slots), f32),
            pltpu.VMEM((mem_dev * MODES, slots), f32),
            pltpu.VMEM((n_lon, 8, size + 128), f32),
            pltpu.VMEM((n_lon, 8, size + 128), f32),
            pltpu.VMEM((n_mem, n_lon, 8, size + 128), f32),
            dma((n_lon - 1,)), dma((n_lon - 1,)),
            dma((n_lon - 1,)), dma((n_lon - 1,)),
            dma((n_mem - 1,)), dma((n_mem - 1,)),
        ],
        compiler_params=params(2),
        name="gram",
    )(
        obs_prior, obs_horiz, level, vert_modes, obs_count,
        obs_value.reshape(1, slots), obs_var.reshape(1, slots),
    )
    anywhere = pl.BlockSpec(memory_space=pl.ANY)
    weights, prior_out = pl.pallas_call(
        solve_kernel,
        out_shape=(
            jax.ShapeDtypeStruct((size, 128), f32),
            jax.ShapeDtypeStruct(prior.shape, f32),
        ),
        in_specs=[vmem(), vmem()],
        out_specs=(vmem(), anywhere),
        scratch_shapes=[pltpu.VMEM((size, size + 128), f32), dma],
        compiler_params=params(),
        name="solve",
    )(system, prior)
    analysis = pl.pallas_call(
        functools.partial(analysis_kernel, n_mem, mem_dev, norm),
        out_shape=jax.ShapeDtypeStruct((layers, width, lats), f32),
        in_specs=[vmem()] * 4 + [smem()],
        out_specs=vmem(),
        scratch_shapes=[
            pltpu.VMEM((n_mem, layers, width, lats), f32),
            dma((layers, n_mem - 1)), dma((layers, n_mem - 1)),
        ],
        compiler_params=params(3),
        name="analysis",
    )(weights, prior, mean, horiz_modes, vert_modes)
    return prior_out.reshape(members.shape), analysis


def padded(block, sides, width):
    for axis, dim in sides:
        count = lax.axis_size(axis)
        forward = [(i, i + 1) for i in range(count - 1)]
        forward.append((count - 1, 0))
        backward = [(target, source) for source, target in forward]
        low = lax.ppermute(
            lax.slice_in_dim(block, block.shape[dim] - width, None, axis=dim), axis, forward
        )
        high = lax.ppermute(lax.slice_in_dim(block, 0, width, axis=dim), axis, backward)
        block = jnp.concatenate([low, block, high], axis=dim)
    return block


def update(centre, western, eastern, flow_lon, flow_lat):
    zero_col = jnp.zeros_like(centre[..., :1])
    south_boundary = jnp.concatenate([zero_col, centre[..., :-1]], axis=-1)
    northern = jnp.concatenate([centre[..., 1:], zero_col], axis=-1)
    result = centre - jnp.maximum(flow_lon, 0.0) * (centre - western)
    result = result - jnp.minimum(flow_lon, 0.0) * (eastern - centre)
    result = result - jnp.maximum(flow_lat, 0.0) * (centre - south_boundary)
    result = result - jnp.minimum(flow_lat, 0.0) * (northern - centre)
    return result


def per_device(
    members,
    courant_lon,
    courant_lat,
    vert_modes,
    horiz_modes,
    obs_index,
    obs_count,
    obs_value,
    obs_var,
):
    mem_dev, layer_tally, band_width, lat_rows = members.shape
    sample_tally_overall = mem_dev * lax.axis_size("mem")
    rim_depth = ADV_STEPS
    stacked = jnp.concatenate(
        [members.reshape(mem_dev * layer_tally, band_width, lat_rows), courant_lon, courant_lat],
        axis=0,
    )
    extended = padded(stacked, (("lon", 1),), rim_depth)
    split_at = mem_dev * layer_tally
    prognostic_vector = extended[:split_at].reshape(
        mem_dev, layer_tally, band_width + 2 * rim_depth, lat_rows
    )
    flow_lon_ext = extended[split_at : split_at + layer_tally]
    meridional_wind_padded = extended[split_at + layer_tally :]
    for section in range(rim_depth):
        out_cols = band_width + 2 * (rim_depth - 1 - section)
        first_col = section + 1
        prognostic_vector = update(
            prognostic_vector[:, :, 1 : out_cols + 1],
            prognostic_vector[:, :, 0:out_cols],
            prognostic_vector[:, :, 2 : out_cols + 2],
            flow_lon_ext[:, first_col : first_col + out_cols],
            meridional_wind_padded[:, first_col : first_col + out_cols],
        )
    sample_centroid = lax.psum(jnp.sum(prognostic_vector, axis=0), "mem") / sample_tally_overall
    sample_departure = prognostic_vector - sample_centroid[None]
    norm_scale = (sample_tally_overall - 1) ** (-0.5)
    obs_slots = obs_index.shape[0]
    band_cells = band_width * lat_rows
    level_idx = obs_index // band_cells
    within = obs_index % band_cells
    anomaly_obs = jnp.take(sample_departure.reshape(mem_dev, -1), obs_index, axis=1)
    mean_obs = jnp.take(sample_centroid.reshape(-1), obs_index)
    vert_obs = jnp.take(vert_modes, level_idx, axis=1)
    horiz_obs = jnp.take(horiz_modes.reshape(KH, -1), within, axis=1)
    modes_obs = (vert_obs[:, None, :] * horiz_obs[None, :, :]).reshape(KV * KH, obs_slots)
    live_mask = (jnp.arange(obs_slots, dtype=jnp.int32) < obs_count[0]).astype(jnp.float32)
    obs_perts = (
        anomaly_obs[:, None, :] * modes_obs[None, :, :] * (live_mask * norm_scale)[None, None, :]
    )
    obs_perts = obs_perts.reshape(mem_dev * KV * KH, obs_slots)
    inv_var = live_mask / obs_var
    innovation = obs_value - mean_obs
    all_perts = lax.all_gather(obs_perts, "mem", axis=0, tiled=True)
    gram_part = jnp.dot(all_perts * inv_var[None, :], all_perts.T, precision=lax.Precision.HIGHEST)
    side_part = jnp.dot(all_perts, inv_var * innovation, precision=lax.Precision.HIGHEST)
    gram_matrix, right_side = lax.psum((gram_part, side_part), "lon")
    system = jnp.eye(gram_matrix.shape[0], dtype=jnp.float32) + gram_matrix
    factor = jnp.linalg.cholesky(system)
    weights = jax.scipy.linalg.cho_solve((factor, True), right_side)
    w_mat = weights.reshape(sample_tally_overall, KV * KH)
    w_local = lax.dynamic_slice_in_dim(w_mat, lax.axis_index("mem") * mem_dev, mem_dev, 0)
    mode_coef = jnp.einsum(
        "mk,mlij->klij", w_local, sample_departure, precision=lax.Precision.HIGHEST
    )
    mode_coef = mode_coef.reshape(KV, KH, layer_tally, band_width, lat_rows)
    inc_part = (
        jnp.einsum(
            "al,bij,ablij->lij", vert_modes, horiz_modes, mode_coef, precision=lax.Precision.HIGHEST
        )
        * norm_scale
    )
    posterior_adjustment = lax.psum(inc_part, "mem")
    return (prognostic_vector, sample_centroid + posterior_adjustment)


def choose(*args):
    mem_dev, layers, width, lats = args[0].shape
    n_lon = lax.axis_size("lon")
    fits = (
        mem_dev == 8
        and layers == 4
        and width % 8 == 0
        and lats % 128 == 0
        and args[5].shape[0] % 512 == 0
        and n_lon > 2
        and mem_dev * MODES == 8 * n_lon
        and (mem_dev * lax.axis_size("mem") * MODES) % 128 == 0
    )
    return fast_device(*args) if fits else per_device(*args)


def solution(mesh):
    placed = (
        P("mem", None, "lon", None),
        P(None, "lon", None),
        P(None, "lon", None),
        P(),
        P(None, "lon", None),
        P("lon"),
        P("lon"),
        P("lon"),
        P("lon"),
    )
    return jax.shard_map(
        choose,
        mesh=mesh,
        in_specs=placed,
        out_specs=(P("mem", None, "lon", None), P(None, "lon", None)),
        check_vma=False,
    )
```
